512 devices in a mesh: tm: 32 (over z, core), net: 16 (over y, x).
Axes of the slice: x: 4, y: 4, z: 16, core: 2. Of those that a mesh axis runs over, the one named last changes fastest.
Arguments:
- ptdf: bfloat16 [16384, 4096], P('net'), may hold values from -0.09375 to 0.09375
- demand: float32 [4096, 2048], P('net', 'tm'), may hold values from 0 to 2
- generation: float32 [4096, 2048], P('net', 'tm'), may hold values from 0 to 2
- cost: float32 [4096, 2048], P('net', 'tm'), may hold values from 0.2 to 4
- gen_cap: float32 [4096], P('net'), may hold values from 0.5 to 4
- storage: float32 [2048, 2048], P('net', 'tm'), may hold values from -3 to 3
- wear: float32 [2048], P('net'), may hold values from 0.1 to 2
- initial_charge: float32 [2048], P('net'), may hold values from 0 to 2
- leakage: float32 [2048], P('net'), may hold values from 0.00014648438 to 0.05
- line_dual: float32 [16384, 2048], P('net', 'tm'), may hold values from -3 to 3
- line_index: int32 [16384], P('net'), may hold values from 0 to 4095
- rating: float32 [4096], replicated, may hold values from 0.3 to 3
- storage_bus: int32 [2048], replicated, may hold values from 0 to 4095
- balance_dual: float32 [2048], P('tm'), may hold values from -4 to 4
- hour_block: int32 [2048], P('tm'), may hold values from 0 to 23
- block_price: float32 [24], replicated, may hold values from -4 to 4
Outputs:
- generation_next: float32 [4096, 2048], P('net', 'tm')
- storage_next: float32 [2048, 2048], P('net', 'tm')
- charge: float32 [2048, 2048], P('net', 'tm')
- line_dual_next: float32 [16384, 2048], P('net', 'tm')
- balance_price: float32 [2048], P('tm')
The draws below stay inside these ranges and needn't reach their ends.
All inputs are finite; a program needn't handle non-finite values.
Results may differ from the reference program's by a relative error of at most 0.0028.
Values may be sent and summed in bfloat16 or wider, within the bound.
No kernel may reach another device: no remote copies, remote signals or barrier semaphores. Data moves between devices by JAX's collectives and lax.ppermute only.
A program may use at most 64 MiB of HBM per device.

```python
import math
import jax
import jax.numpy as jnp
from jax import lax

NB = 4096
L = 16384
S = 2048
LINES = 4096
BLOCKS = 24
PASSES = 2
H = 2048


def plant(array, key, least, largest):
    place = [jax.random.randint(jax.random.fold_in(key, axis), (), 0, length) for axis, length in enumerate(array.shape)]
    longest = array.shape.index(max(array.shape))
    neighbour = place[:longest] + [(place[longest] + 1) % array.shape[longest]] + place[longest + 1:]
    return array.at[tuple(place)].set(least).at[tuple(neighbour)].set(largest)


def block_levels(stream_key, dims, cuts, least, top_value):
    def one(dim, blocks):
        heights = jax.random.uniform(jax.random.fold_in(jax.random.fold_in(stream_key, 6), dim), (blocks,), jnp.float32, least / len(cuts), top_value / len(cuts))
        return jnp.repeat(jnp.exp(heights), dims[dim] // blocks).reshape((-1,) + (1,) * (len(dims) - dim - 1))

    gain = one(*cuts[0])
    for cut in cuts[1:]:
        gain = gain * one(*cut)
    return gain


def centred(key, dims, scale, most, cuts=(), dtype=jnp.bfloat16):
    factor_of = block_levels(key, dims, cuts, -0.22, 0.18) if cuts else 1.0
    array = jax.random.normal(key, dims, jnp.float32) * scale * factor_of
    return jnp.minimum(jnp.maximum(array, -most), most).astype(dtype)


def setup_inputs(seed: int = 0) -> dict:
    key_list = jax.random.split(jax.random.key(seed), 17)
    ptdf = centred(key_list[0], (L, NB), NB ** -0.5, 0.09375, ((0, 16),))
    demand = jnp.clip(2.0 * jax.random.uniform(key_list[1], (NB, H), jnp.float32) ** block_levels(key_list[1], (NB, H), ((0, 16), (1, 32)), -0.2, 0.2), 0.0, 2.0)
    generation = jnp.clip(2.0 * jax.random.uniform(key_list[2], (NB, H), jnp.float32) ** block_levels(key_list[2], (NB, H), ((0, 16), (1, 32)), -0.2, 0.2), 0.0, 2.0)
    cost = jnp.clip(jnp.exp(math.log(4.0) - 2.9957323 * jax.random.uniform(key_list[3], (NB, H), jnp.float32) ** block_levels(key_list[3], (NB, H), ((0, 16), (1, 32)), -0.2, 0.2)), 0.2, 4.0)
    gen_cap = jnp.clip(jnp.exp(math.log(4.0) - 2.0794415 * jax.random.uniform(key_list[4], (NB,), jnp.float32) ** block_levels(key_list[4], (NB,), ((0, 16),), -0.2, 0.2)), 0.5, 4.0)
    storage = centred(key_list[5], (S, H), 0.5, 3.0, ((0, 16), (1, 32)), jnp.float32)
    wear = jnp.clip(jnp.exp(math.log(2.0) - 2.9957323 * jax.random.uniform(key_list[6], (S,), jnp.float32) ** block_levels(key_list[6], (S,), ((0, 16),), -0.2, 0.2)), 0.1, 2.0)
    initial_charge = jnp.clip(2.0 * jax.random.uniform(key_list[7], (S,), jnp.float32) ** block_levels(key_list[7], (S,), ((0, 16),), -0.2, 0.2), 0.0, 2.0)
    leakage = jnp.clip(jnp.exp(math.log(0.05) - 5.8328595 * jax.random.uniform(key_list[8], (S,), jnp.float32) ** block_levels(key_list[8], (S,), ((0, 16),), -0.2, 0.2)), 0.00014648438, 0.05)
    line_dual = centred(key_list[9], (L, H), 0.3, 3.0, ((0, 16), (1, 32)), jnp.float32)
    line_index = plant(jax.random.randint(key_list[10], (L,), 0, LINES), jax.random.fold_in(key_list[10], 1), 0, LINES - 1).astype(jnp.int32)
    rating = jnp.clip(jnp.exp(jax.random.uniform(key_list[11], (LINES,), jnp.float32, math.log(0.3), math.log(3.0))), 0.3, 3.0)
    storage_bus = plant(jax.random.randint(key_list[12], (S,), 0, NB), jax.random.fold_in(key_list[12], 1), 0, NB - 1).astype(jnp.int32)
    balance_dual = centred(key_list[13], (H,), 1.0, 4.0, ((0, 32),), jnp.float32)
    hour_block = plant(jax.random.randint(key_list[14], (H,), 0, BLOCKS), jax.random.fold_in(key_list[14], 1), 0, BLOCKS - 1).astype(jnp.int32)
    block_price = centred(key_list[15], (BLOCKS,), 1.0, 4.0, (), jnp.float32)
    return {"ptdf": ptdf, "demand": demand, "generation": generation, "cost": cost, "gen_cap": gen_cap, "storage": storage, "wear": wear, "initial_charge": initial_charge, "leakage": leakage, "line_dual": line_dual, "line_index": line_index, "rating": rating, "storage_bus": storage_bus, "balance_dual": balance_dual, "hour_block": hour_block, "block_price": block_price}


STEP = 0.1
BAL = 0.5
STEP_UNIT = 0.2
ETA = 0.0625


def product(left, right):
    return jnp.dot(left.astype(jnp.float32), right.astype(jnp.float32), precision=lax.Precision.HIGHEST)


def reference(ptdf, demand, generation, cost, gen_cap, storage, wear, initial_charge, leakage, line_dual, line_index, rating, storage_bus, balance_dual, hour_block, block_price):
    limit = rating[line_index][:, None]
    unit_columns = ptdf[:, storage_bus]
    unit_flow = product(unit_columns, storage.astype(jnp.bfloat16))
    unit_total = jnp.sum(storage, axis=0)
    gen = generation
    dual = line_dual
    price = balance_dual
    for turn in range(PASSES):
        injection = (gen - demand).astype(jnp.bfloat16)
        flows = product(ptdf, injection) + unit_flow
        shifted = flows + dual
        dual = shifted - jnp.clip(shifted, -limit, limit)
        pull = product(ptdf.T, dual.astype(jnp.bfloat16))
        trial = jnp.clip(gen - STEP * (cost - price[None, :] + pull), 0.0, gen_cap[:, None])
        mismatch = jnp.sum(trial - demand, axis=0) + unit_total
        gen = trial - mismatch[None, :] / NB
        price = price - BAL * mismatch / NB
    hour_price = block_price[hour_block]
    storage_next = jnp.clip(storage + STEP_UNIT * (price[None, :] + hour_price[None, :] - wear[:, None] * storage), -1.0, 1.0)
    keep = 1.0 - leakage

    def advance(carry, column):
        carry = keep * carry - ETA * column
        return carry, carry

    _, charge = lax.scan(advance, initial_charge, storage_next.T)
    return gen, storage_next, charge.T, dual, price
```

```python
import jax
import jax.numpy as jnp
from jax import lax
from jax.experimental import pallas as pl
from jax.experimental.pallas import tpu as pltpu
from jax.sharding import Mesh
from jax.sharding import PartitionSpec as P

TM = ("tm_0", "tm_1")

STEP = 0.1
BAL = 0.5
STEP_UNIT = 0.2
ETA = 0.0625

F32 = jnp.float32
BF16 = jnp.bfloat16
NT = (((1,), (1,)), ((), ()))


def call(kernel, name, *outs):
    return pl.pallas_call(
        kernel,
        name=name,
        out_shape=tuple(jax.ShapeDtypeStruct(s, d) for s, d in outs),
        compiler_params=pltpu.CompilerParams(vmem_limit_bytes=48 << 20),
    )


def shape(s, d):
    return s, d


def iota(dims, axis):
    return lax.broadcasted_iota(jnp.int32, dims, axis)


def column(row, n):
    eye = iota((n, n), 0) == iota((n, n), 1)
    return jnp.sum(jnp.where(eye, row[:, :n], jnp.zeros((), row.dtype)), axis=1, keepdims=True)


def row_of(col, width):
    n = col.shape[0]
    eye = iota((n, width), 0) == iota((n, width), 1)
    return jnp.sum(jnp.where(eye, col, 0.0), axis=0, keepdims=True)


def three_parts(value):
    high = value.astype(BF16)
    rest = value - high.astype(F32)
    middle = rest.astype(BF16)
    low = (rest - middle.astype(F32)).astype(BF16)
    return high, middle, low


def pack_body(gen, demand, storage, out):
    rows = gen.shape[1]
    injection = (gen[...] - demand[...]).astype(BF16)
    units = storage[...].astype(BF16)
    for d in range(out.shape[0]):
        out[d, :, :rows] = injection
        out[d, :, rows:] = units


def tables_body(rating, index, leakage, hour_block, block_price, limit, growth, hour_price):
    groups = rating.shape[0]
    at = index[...]
    hot = (iota((groups, at.shape[1]), 0) == at // 128).astype(BF16)
    table = rating[...].T
    picked = sum(jnp.dot(part, hot, preferred_element_type=F32) for part in three_parts(table))
    here = iota((128, at.shape[1]), 0) == at % 128
    limit[...] = jnp.sum(jnp.where(here, picked, 0.0), axis=0, keepdims=True)
    hours, units = growth.shape
    offsets = (iota((hours, units), 0) + 1).astype(F32)
    growth[...] = jnp.exp(offsets * jnp.log(1.0 - leakage[...]))
    block = column(hour_block[...], hours)
    blocks = block_price.shape[1]
    price = jnp.where(block == iota((hours, blocks), 1), block_price[...], 0.0)
    hour_price[...] = jnp.broadcast_to(jnp.sum(price, axis=1, keepdims=True), hour_price.shape)


def clipped(flows, dual, limit):
    shifted = flows + dual
    return shifted - jnp.clip(shifted, -limit, limit)


def pull_parts(dual, ptdf, out):
    pull = jnp.dot(dual.astype(BF16), ptdf[...], preferred_element_type=F32)
    rows = out.shape[2]
    for d in range(out.shape[0]):
        out[d] = pull[:, d * rows : (d + 1) * rows].astype(BF16)


def first_body(arrived, ptdf, line_dual, limit, bus, parts, dual_out, unit_flow_out):
    count, hours, width = arrived.shape
    rows = parts.shape[2]
    units = width - rows
    spread = jnp.zeros((count * hours, rows), F32)
    for k in range(0, count, 2):
        at = bus[:, k * units : (k + 2) * units]
        owner, place = at // rows, at % rows
        storage = jnp.concatenate([arrived[k, :, rows:], arrived[k + 1, :, rows:]], axis=1)
        hot = (iota((rows, 2 * units), 0) == place).astype(F32).astype(BF16)
        owned = [
            storage * jnp.broadcast_to((owner == d).astype(F32), storage.shape).astype(BF16)
            for d in range(count)
        ]
        spread += lax.dot_general(
            jnp.concatenate(owned, axis=0), hot, NT, preferred_element_type=F32
        )
    lefts = []
    for d in range(count):
        part = spread[d * hours : (d + 1) * hours]
        high = part.astype(BF16)
        low = (part - high.astype(F32)).astype(BF16)
        lefts.append(jnp.concatenate([arrived[d, :, :rows], high, low], axis=0))
    products = lax.dot_general(
        jnp.concatenate(lefts, axis=1), ptdf[...], NT, preferred_element_type=F32
    )
    unit_flow = products[hours : 2 * hours] + products[2 * hours :]
    unit_flow_out[...] = unit_flow
    dual = clipped(products[:hours] + unit_flow, line_dual[...], limit[...])
    dual_out[...] = dual
    pull_parts(dual, ptdf, parts)


def second_body(arrived, ptdf, line_dual, limit, unit_flow, parts, dual_out, mean_out):
    count, rows = parts.shape[0], parts.shape[2]
    hours = parts.shape[1]
    total = arrived[0, :hours]
    extra = arrived[0, hours : hours + 1]
    for d in range(1, count):
        total += arrived[d, :hours]
        extra += arrived[d, hours : hours + 1]
    mismatch = jnp.sum(total, axis=1, keepdims=True) + column(extra, hours)
    mean = mismatch / (count * rows)
    mean_out[...] = jnp.broadcast_to(mean, mean_out.shape)
    injection = [(arrived[d, :hours] - mean).astype(BF16) for d in range(count)]
    flows = lax.dot_general(
        jnp.concatenate(injection, axis=1), ptdf[...], NT, preferred_element_type=F32
    )
    dual = clipped(flows + unit_flow[...], line_dual[...], limit[...])
    dual_out[...] = dual
    pull_parts(dual, ptdf, parts)


def total_of(arrived):
    total = arrived[0].astype(F32)
    for d in range(1, arrived.shape[0]):
        total += arrived[d].astype(F32)
    return total


def trial_body(arrived, gen, cost, demand, price, cap, storage, send, trial_out):
    hours = gen.shape[0]
    pull = total_of(arrived)
    now = column(price[...], hours)
    trial = jnp.clip(gen[...] - STEP * (cost[...] - now + pull), 0.0, cap[...])
    trial_out[...] = trial
    balance = trial - demand[...]
    unit_sum = row_of(jnp.sum(storage[...], axis=1, keepdims=True), send.shape[2])
    below = jnp.broadcast_to(unit_sum, (send.shape[1] - hours, send.shape[2]))
    for d in range(send.shape[0]):
        send[d, :hours] = balance
        send[d, hours:] = below


def last_trial_body(arrived, before, mean, cost, demand, price, cap, storage, send, trial_out):
    hours = before.shape[0]
    pull = total_of(arrived)
    moved = mean[:, :1]
    now = column(price[...], hours) - BAL * moved
    trial = jnp.clip(before[...] - moved - STEP * (cost[...] - now + pull), 0.0, cap[...])
    trial_out[...] = trial
    own = jnp.sum(trial - demand[...], axis=1, keepdims=True)
    own += jnp.sum(storage[...], axis=1, keepdims=True)
    send[...] = jnp.broadcast_to(row_of(own, send.shape[2])[None], send.shape)


def finish_body(
    arrived, trial, mean, price, hour_price, storage, wear, growth, gen_out, storage_out, running_out, price_out, last_out
):
    hours, units = storage.shape
    buses = arrived.shape[0] * trial.shape[1]
    mismatch = column(total_of(arrived)[:1], hours) / buses
    gen_out[...] = trial[...] - mismatch
    now = column(price[...], hours) - BAL * mean[:, :1] - BAL * mismatch
    price_out[...] = row_of(now, price_out.shape[1])
    held = storage[...]
    nexts = jnp.clip(held + STEP_UNIT * (now + hour_price[...] - wear[...] * held), -1.0, 1.0)
    storage_out[...] = nexts
    running = -ETA * nexts
    hour = iota((hours, units), 0)
    span = 1
    while span < hours:
        moved = jnp.where(hour >= span, pltpu.roll(running, span, 0), 0.0)
        running = running + growth[span - 1 : span] * moved
        span *= 2
    running_out[...] = running
    last_out[...] = jnp.broadcast_to(running[hours - 1 :], last_out.shape)


def chip_body(pair, growth, send):
    hours = growth.shape[0]
    both = growth[hours - 1 :] * pair[0] + pair[1]
    send[...] = jnp.broadcast_to(both[None], send.shape)


def charge_body(here, arrived, pair, growth, initial, running, charge):
    hours = growth.shape[0]
    keep = growth[hours - 1 :]
    twice = keep * keep
    entering = initial[...]
    for k in range(arrived.shape[0]):
        entering = jnp.where(k < here[0], twice * entering + arrived[k, :1], entering)
    entering = jnp.where(here[1] > 0, keep * entering + pair[0, :1], entering)
    charge[...] = growth[...] * entering + running[...]


def everywhere(blocks, axis):
    return lax.all_to_all(blocks, axis, split_axis=0, concat_axis=0, tiled=True)


def per_device(
    ptdf,
    demand,
    generation,
    cost,
    gen_cap,
    storage,
    wear,
    initial_charge,
    leakage,
    line_dual,
    line_index,
    rating,
    storage_bus,
    balance_dual,
    hour_block,
    block_price,
):
    net = lax.axis_size("net")
    chips = lax.axis_size("tm_0")
    lines = ptdf.shape[0]
    rows, hours = generation.shape
    units = storage.shape[0]
    demand, gen, cost, held = demand.T, generation.T, cost.T, storage.T
    dual = line_dual.T
    cap, wear, initial = gen_cap[None], wear[None], initial_charge[None]
    price = balance_dual[None]
    (packed,) = call(pack_body, "pack", shape((net, hours, rows + units), BF16))(gen, demand, held)
    arrived = everywhere(packed, "net")
    limit, growth, hour_price = call(
        tables_body,
        "tables",
        shape((1, lines), F32),
        shape((hours, units), F32),
        shape((hours, units), F32),
    )(rating.reshape(-1, 128), line_index[None], leakage[None], hour_block[None], block_price[None])
    parts, dual, unit_flow = call(
        first_body,
        "first",
        shape((net, hours, rows), BF16),
        shape((hours, lines), F32),
        shape((hours, lines), F32),
    )(arrived, ptdf, dual, limit, storage_bus[None])
    arrived = everywhere(parts, "net")
    send, trial = call(
        trial_body, "trial", shape((net, hours + 8, rows), F32), shape((hours, rows), F32)
    )(arrived, gen, cost, demand, price, cap, held)
    arrived = everywhere(send, "net")
    parts, dual, mean = call(
        second_body,
        "second",
        shape((net, hours, rows), BF16),
        shape((hours, lines), F32),
        shape((hours, 128), F32),
    )(arrived, ptdf, dual, limit, unit_flow)
    arrived = everywhere(parts, "net")
    send, trial = call(
        last_trial_body, "last_trial", shape((net, 8, 128), F32), shape((hours, rows), F32)
    )(arrived, trial, mean, cost, demand, price, cap, held)
    arrived = everywhere(send, "net")
    gen, storage_next, running, price, last = call(
        finish_body,
        "finish",
        shape((hours, rows), F32),
        shape((hours, units), F32),
        shape((hours, units), F32),
        shape((1, hours), F32),
        shape((8, units), F32),
    )(arrived, trial, mean, price, hour_price, held, wear, growth)
    pair = lax.all_gather(last, "tm_1")
    (send,) = call(chip_body, "chip", shape((chips, 8, units), F32))(pair, growth)
    arrived = everywhere(send, "tm_0")
    here = jnp.stack([lax.axis_index("tm_0"), lax.axis_index("tm_1")])
    smem = pl.BlockSpec(memory_space=pltpu.SMEM)
    vmem = pl.BlockSpec(memory_space=pltpu.VMEM)
    charge = pl.pallas_call(
        charge_body,
        name="charge",
        in_specs=[smem] + [vmem] * 5,
        out_shape=jax.ShapeDtypeStruct((hours, units), F32),
    )(here, arrived, pair, growth, initial, running)
    return (gen.T, storage_next.T, charge.T, dual.T, price[0])


def solution(mesh):
    split = Mesh(mesh.devices.reshape(16, 2, mesh.shape["net"]), ("tm_0", "tm_1", "net"))
    in_specs = (
        P("net", None),
        P("net", TM),
        P("net", TM),
        P("net", TM),
        P("net"),
        P("net", TM),
        P("net"),
        P("net"),
        P("net"),
        P("net", TM),
        P("net"),
        P(),
        P(),
        P(TM),
        P(TM),
        P(),
    )
    out_specs = (P("net", TM), P("net", TM), P("net", TM), P("net", TM), P(TM))
    return jax.shard_map(
        per_device, mesh=split, in_specs=in_specs, out_specs=out_specs, check_vma=False
    )
```

```python
import jax
import jax.numpy as jnp
from jax import lax
from jax.experimental import pallas as pl
from jax.experimental.pallas import tpu as pltpu
from jax.sharding import Mesh
from jax.sharding import PartitionSpec as P

TM = ("tm_0", "tm_1")

STEP = 0.1
BAL = 0.5
STEP_UNIT = 0.2
ETA = 0.0625

F32 = jnp.float32
VMEM_LIMIT = 16 << 20
CHUNKS = 4
BF16 = jnp.bfloat16
NT = (((1,), (1,)), ((), ()))


def call(kernel, name, *outs):
    return pl.pallas_call(
        kernel,
        name=name,
        out_shape=tuple(jax.ShapeDtypeStruct(s, d) for s, d in outs),
        compiler_params=pltpu.CompilerParams(vmem_limit_bytes=VMEM_LIMIT),
    )


def shape(s, d):
    return s, d


def iota(dims, axis):
    return lax.broadcasted_iota(jnp.int32, dims, axis)


def column(row, n):
    eye = iota((n, n), 0) == iota((n, n), 1)
    return jnp.sum(jnp.where(eye, row[:, :n], jnp.zeros((), row.dtype)), axis=1, keepdims=True)


def row_of(col, width):
    n = col.shape[0]
    eye = iota((n, width), 0) == iota((n, width), 1)
    return jnp.sum(jnp.where(eye, col, 0.0), axis=0, keepdims=True)


def three_parts(value):
    high = value.astype(BF16)
    rest = value - high.astype(F32)
    middle = rest.astype(BF16)
    low = (rest - middle.astype(F32)).astype(BF16)
    return high, middle, low


def pack_body(gen_in, demand_in, storage_in, out, gen, demand, storage, sems):
    pairs = ((gen_in, gen), (demand_in, demand), (storage_in, storage))
    copies = [pltpu.make_async_copy(a, b, sems.at[k]) for k, (a, b) in enumerate(pairs)]
    for copy in copies:
        copy.start()
    for copy in copies:
        copy.wait()
    rows = gen.shape[1]
    injection = (gen[...] - demand[...]).astype(BF16)
    units = storage[...].astype(BF16)
    for d in range(out.shape[0]):
        out[d, :, :rows] = injection
        out[d, :, rows:] = units


def write_tables(
    here, rating, index, leakage, hour_block, block_price, initial, limit, growth, hour_price, chain
):
    groups = rating.shape[0]
    at = index[...]
    hot = (iota((groups, at.shape[1]), 0) == at // 128).astype(BF16)
    table = rating[...].T
    picked = sum(jnp.dot(part, hot, preferred_element_type=F32) for part in three_parts(table))
    found = iota((128, at.shape[1]), 0) == at % 128
    limit[...] = jnp.sum(jnp.where(found, picked, 0.0), axis=0, keepdims=True)
    hours, units = growth.shape
    offsets = (iota((hours, units), 0) + 1).astype(F32)
    rate = jnp.log(1.0 - leakage[...])
    growth[...] = jnp.exp(offsets * rate)
    count = chain.shape[0] - 8
    row = iota(chain.shape, 0)
    spans = jnp.where(row < count, 2 * (here[0] - 1 - row), 2 * here[0]) + here[1]
    weight = jnp.exp((jnp.maximum(spans, 0) * hours).astype(F32) * rate)
    weight = jnp.where((row < here[0]) | (row == count), weight, 0.0)
    weight = jnp.where(row == count, weight * initial[...], weight)
    chain[...] = jnp.where(row == count + 1, here[1].astype(F32), weight)
    block = column(hour_block[...], hours)
    blocks = block_price.shape[1]
    price = jnp.where(block == iota((hours, blocks), 1), block_price[...], 0.0)
    hour_price[...] = jnp.broadcast_to(jnp.sum(price, axis=1, keepdims=True), hour_price.shape)


def clipped(flows, dual, limit):
    shifted = flows + dual
    return shifted - jnp.clip(shifted, -limit, limit)


def pull_parts(dual, ptdf, out):
    pull = jnp.dot(dual.astype(BF16), ptdf[...], preferred_element_type=F32)
    rows = out.shape[2]
    for d in range(out.shape[0]):
        out[d] = pull[:, d * rows : (d + 1) * rows].astype(BF16)


def first_body(
    here, arrived, ptdf, line_dual, bus, rating, index, leakage, hour_block, block_price, initial,
    parts, dual_out, unit_flow_out, limit, growth, hour_price, chain, held, lefts, sems
):
    chunk = held.shape[0] // CHUNKS
    spans = [pl.ds(k * chunk, chunk) for k in range(CHUNKS)]
    copies = [
        pltpu.make_async_copy(ptdf.at[at], held.at[at], sems.at[k]) for k, at in enumerate(spans)
    ]
    for copy in copies:
        copy.start()
    write_tables(
        here, rating, index, leakage, hour_block, block_price, initial, limit, growth, hour_price, chain
    )
    count, hours, width = arrived.shape
    rows = parts.shape[2]
    units = width - rows
    spread = jnp.zeros((count * hours, rows), F32)
    for k in range(0, count, 2):
        at = bus[:, k * units : (k + 2) * units]
        owner, place = at // rows, at % rows
        storage = jnp.concatenate([arrived[k, :, rows:], arrived[k + 1, :, rows:]], axis=1)
        hot = (iota((rows, 2 * units), 0) == place).astype(F32).astype(BF16)
        owned = [
            storage * jnp.broadcast_to((owner == d).astype(F32), storage.shape).astype(BF16)
            for d in range(count)
        ]
        spread += lax.dot_general(
            jnp.concatenate(owned, axis=0), hot, NT, preferred_element_type=F32
        )
    for d in range(count):
        part = spread[d * hours : (d + 1) * hours]
        high = part.astype(BF16)
        at = slice(d * rows, (d + 1) * rows)
        lefts[:hours, at] = arrived[d, :, :rows]
        lefts[hours : 2 * hours, at] = high
        lefts[2 * hours :, at] = (part - high.astype(F32)).astype(BF16)
    for copy, at in zip(copies, spans):
        copy.wait()
        products = lax.dot_general(lefts[...], held[at], NT, preferred_element_type=F32)
        unit_flow = products[hours : 2 * hours] + products[2 * hours :]
        unit_flow_out[:, at] = unit_flow
        dual_out[:, at] = clipped(products[:hours] + unit_flow, line_dual[:, at], limit[:, at])
    pull_parts(dual_out[...], held, parts)


def second_body(arrived, ptdf, line_dual, limit, unit_flow, parts, dual_out, mean_out):
    count, rows = parts.shape[0], parts.shape[2]
    hours = parts.shape[1]
    total = arrived[0, :hours]
    extra = arrived[0, hours : hours + 1]
    for d in range(1, count):
        total += arrived[d, :hours]
        extra += arrived[d, hours : hours + 1]
    mismatch = jnp.sum(total, axis=1, keepdims=True) + column(extra, hours)
    mean = mismatch / (count * rows)
    mean_out[...] = jnp.broadcast_to(mean, mean_out.shape)
    injection = [(arrived[d, :hours] - mean).astype(BF16) for d in range(count)]
    flows = lax.dot_general(
        jnp.concatenate(injection, axis=1), ptdf[...], NT, preferred_element_type=F32
    )
    dual = clipped(flows + unit_flow[...], line_dual[...], limit[...])
    dual_out[...] = dual
    pull_parts(dual, ptdf, parts)


def total_of(arrived):
    total = arrived[0].astype(F32)
    for d in range(1, arrived.shape[0]):
        total += arrived[d].astype(F32)
    return total


def trial_body(arrived, gen, cost, demand, price, cap, storage, send, trial_out):
    hours = gen.shape[0]
    pull = total_of(arrived)
    now = column(price[...], hours)
    trial = jnp.clip(gen[...] - STEP * (cost[...] - now + pull), 0.0, cap[...])
    trial_out[...] = trial
    balance = trial - demand[...]
    unit_sum = row_of(jnp.sum(storage[...], axis=1, keepdims=True), send.shape[2])
    below = jnp.broadcast_to(unit_sum, (send.shape[1] - hours, send.shape[2]))
    for d in range(send.shape[0]):
        send[d, :hours] = balance
        send[d, hours:] = below


def last_trial_body(arrived, before, mean, cost, demand, price, cap, storage, send, trial_out):
    hours = before.shape[0]
    pull = total_of(arrived)
    moved = mean[:, :1]
    now = column(price[...], hours) - BAL * moved
    trial = jnp.clip(before[...] - moved - STEP * (cost[...] - now + pull), 0.0, cap[...])
    trial_out[...] = trial
    own = jnp.sum(trial - demand[...], axis=1, keepdims=True)
    own += jnp.sum(storage[...], axis=1, keepdims=True)
    send[...] = jnp.broadcast_to(row_of(own, send.shape[2])[None], send.shape)


def finish_body(
    arrived, trial, mean, price, hour_price, storage, wear, growth, gen_out, storage_out, running_out, price_out, last_out
):
    hours, units = storage.shape
    buses = arrived.shape[0] * trial.shape[1]
    mismatch = column(total_of(arrived)[:1], hours) / buses
    gen_out[...] = trial[...] - mismatch
    now = column(price[...], hours) - BAL * mean[:, :1] - BAL * mismatch
    price_out[...] = row_of(now, price_out.shape[1])
    held = storage[...]
    nexts = jnp.clip(held + STEP_UNIT * (now + hour_price[...] - wear[...] * held), -1.0, 1.0)
    storage_out[...] = nexts
    running = -ETA * nexts
    hour = iota((hours, units), 0)
    span = 1
    while span < hours:
        moved = jnp.where(hour >= span, pltpu.roll(running, span, 0), 0.0)
        running = running + growth[span - 1 : span] * moved
        span *= 2
    running_out[...] = running
    last_out[...] = jnp.broadcast_to(running[hours - 1 :], last_out.shape)


def chip_body(pair, growth, send):
    hours = growth.shape[0]
    both = growth[hours - 1 :] * pair[0] + pair[1]
    send[...] = jnp.broadcast_to(both[None], send.shape)


def charge_body(arrived, pair, growth, chain, running, charge):
    count = arrived.shape[0]
    entering = chain[count : count + 1] + chain[count + 1 : count + 2] * pair[0, :1]
    for k in range(count):
        entering += chain[k : k + 1] * arrived[k, :1]
    charge[...] = growth[...] * entering + running[...]


def everywhere(blocks, axis):
    return lax.all_to_all(blocks, axis, split_axis=0, concat_axis=0, tiled=True)


def per_device(
    ptdf,
    demand,
    generation,
    cost,
    gen_cap,
    storage,
    wear,
    initial_charge,
    leakage,
    line_dual,
    line_index,
    rating,
    storage_bus,
    balance_dual,
    hour_block,
    block_price,
):
    net = lax.axis_size("net")
    chips = lax.axis_size("tm_0")
    lines = ptdf.shape[0]
    rows, hours = generation.shape
    units = storage.shape[0]
    demand, gen, cost, held = demand.T, generation.T, cost.T, storage.T
    dual = line_dual.T
    cap, wear, initial = gen_cap[None], wear[None], initial_charge[None]
    price = balance_dual[None]
    here = jnp.stack([lax.axis_index("tm_0"), lax.axis_index("tm_1")])
    here, gen = lax.optimization_barrier((here, gen))
    packed = pl.pallas_call(
        pack_body,
        name="pack",
        in_specs=[pl.BlockSpec(memory_space=pltpu.HBM)] * 3,
        out_shape=jax.ShapeDtypeStruct((net, hours, rows + units), BF16),
        scratch_shapes=[
            pltpu.VMEM((hours, rows), F32),
            pltpu.VMEM((hours, rows), F32),
            pltpu.VMEM((hours, units), F32),
            pltpu.SemaphoreType.DMA((3,)),
        ],
        compiler_params=pltpu.CompilerParams(vmem_limit_bytes=VMEM_LIMIT),
    )(*(pltpu.with_memory_space_constraint(a, pltpu.HBM) for a in (gen, demand, held)))
    arrived = everywhere(packed, "net")
    parts, dual, unit_flow, limit, growth, hour_price, chain, kept = pl.pallas_call(
        first_body,
        name="first",
        in_specs=[
            pl.BlockSpec(memory_space=pltpu.SMEM),
            pl.BlockSpec(),
            pl.BlockSpec(memory_space=pltpu.HBM),
        ]
        + [pl.BlockSpec()] * 8,
        out_shape=(
            jax.ShapeDtypeStruct((net, hours, rows), BF16),
            jax.ShapeDtypeStruct((hours, lines), F32),
            jax.ShapeDtypeStruct((hours, lines), F32),
            jax.ShapeDtypeStruct((1, lines), F32),
            jax.ShapeDtypeStruct((hours, units), F32),
            jax.ShapeDtypeStruct((hours, units), F32),
            jax.ShapeDtypeStruct((chips + 8, units), F32),
            jax.ShapeDtypeStruct(ptdf.shape, BF16),
        ),
        scratch_shapes=[
            pltpu.VMEM((3 * hours, net * rows), BF16),
            pltpu.SemaphoreType.DMA((CHUNKS,)),
        ],
        compiler_params=pltpu.CompilerParams(vmem_limit_bytes=VMEM_LIMIT),
    )(
        here,
        arrived,
        pltpu.with_memory_space_constraint(ptdf, pltpu.HBM),
        dual,
        storage_bus[None],
        rating.reshape(-1, 128),
        line_index[None],
        leakage[None],
        hour_block[None],
        block_price[None],
        initial,
    )
    arrived = everywhere(parts, "net")
    send, trial = call(
        trial_body, "trial", shape((net, hours + 8, rows), F32), shape((hours, rows), F32)
    )(arrived, gen, cost, demand, price, cap, held)
    arrived = everywhere(send, "net")
    parts, dual, mean = call(
        second_body,
        "second",
        shape((net, hours, rows), BF16),
        shape((hours, lines), F32),
        shape((hours, 128), F32),
    )(arrived, kept, dual, limit, unit_flow)
    arrived = everywhere(parts, "net")
    send, trial = call(
        last_trial_body, "last_trial", shape((net, 8, 128), F32), shape((hours, rows), F32)
    )(arrived, trial, mean, cost, demand, price, cap, held)
    arrived = everywhere(send, "net")
    gen, storage_next, running, price, last = call(
        finish_body,
        "finish",
        shape((hours, rows), F32),
        shape((hours, units), F32),
        shape((hours, units), F32),
        shape((1, hours), F32),
        shape((8, units), F32),
    )(arrived, trial, mean, price, hour_price, held, wear, growth)
    pair = lax.all_gather(last, "tm_1")
    (send,) = call(chip_body, "chip", shape((chips, 8, units), F32))(pair, growth)
    arrived = everywhere(send, "tm_0")
    (charge,) = call(charge_body, "charge", shape((hours, units), F32))(
        arrived, pair, growth, chain, running
    )
    return (gen.T, storage_next.T, charge.T, dual.T, price[0])


def solution(mesh):
    split = Mesh(mesh.devices.reshape(16, 2, mesh.shape["net"]), ("tm_0", "tm_1", "net"))
    in_specs = (
        P("net", None),
        P("net", TM),
        P("net", TM),
        P("net", TM),
        P("net"),
        P("net", TM),
        P("net"),
        P("net"),
        P("net"),
        P("net", TM),
        P("net"),
        P(),
        P(),
        P(TM),
        P(TM),
        P(),
    )
    out_specs = (P("net", TM), P("net", TM), P("net", TM), P("net", TM), P(TM))
    return jax.shard_map(
        per_device, mesh=split, in_specs=in_specs, out_specs=out_specs, check_vma=False
    )
```

```python
import jax
import jax.numpy as jnp
from jax import lax
from jax.experimental import pallas as pl
from jax.experimental.pallas import tpu as pltpu
from jax.sharding import Mesh
from jax.sharding import PartitionSpec as P

TM = ("tm_0", "tm_1")

STEP = 0.1
BAL = 0.5
STEP_UNIT = 0.2
ETA = 0.0625

F32 = jnp.float32
VMEM_LIMIT = 16 << 20
CHUNKS = 4
BF16 = jnp.bfloat16
NT = (((1,), (1,)), ((), ()))


def call(kernel, name, *outs):
    return pl.pallas_call(
        kernel,
        name=name,
        out_shape=tuple(jax.ShapeDtypeStruct(s, d) for s, d in outs),
        compiler_params=pltpu.CompilerParams(vmem_limit_bytes=VMEM_LIMIT),
    )


def shape(s, d):
    return s, d


def iota(dims, axis):
    return lax.broadcasted_iota(jnp.int32, dims, axis)


def column(row, n):
    eye = iota((n, n), 0) == iota((n, n), 1)
    return jnp.sum(jnp.where(eye, row[:, :n], jnp.zeros((), row.dtype)), axis=1, keepdims=True)


def row_of(col, width):
    n = col.shape[0]
    eye = iota((n, width), 0) == iota((n, width), 1)
    return jnp.sum(jnp.where(eye, col, 0.0), axis=0, keepdims=True)


def three_parts(value):
    high = value.astype(BF16)
    rest = value - high.astype(F32)
    middle = rest.astype(BF16)
    low = (rest - middle.astype(F32)).astype(BF16)
    return high, middle, low


def pack_body(gen_in, demand_in, storage_in, out, gen, demand, storage, sems):
    pairs = ((gen_in, gen), (demand_in, demand), (storage_in, storage))
    copies = [pltpu.make_async_copy(a, b, sems.at[k]) for k, (a, b) in enumerate(pairs)]
    for copy in copies:
        copy.start()
    for copy in copies:
        copy.wait()
    rows = gen.shape[1]
    injection = (gen[...] - demand[...]).astype(BF16)
    units = storage[...].astype(BF16)
    for d in range(out.shape[0]):
        out[d, :, :rows] = injection
        out[d, :, rows:] = units


def write_tables(
    here, rating, index, leakage, hour_block, block_price, initial, limit, growth, hour_price, chain
):
    groups = rating.shape[0]
    at = index[...]
    hot = (iota((groups, at.shape[1]), 0) == at // 128).astype(BF16)
    table = rating[...].T
    picked = sum(jnp.dot(part, hot, preferred_element_type=F32) for part in three_parts(table))
    found = iota((128, at.shape[1]), 0) == at % 128
    limit[...] = jnp.sum(jnp.where(found, picked, 0.0), axis=0, keepdims=True)
    hours, units = growth.shape
    offsets = (iota((hours, units), 0) + 1).astype(F32)
    rate = jnp.log(1.0 - leakage[...])
    growth[...] = jnp.exp(offsets * rate)
    count = chain.shape[0] - 8
    row = iota(chain.shape, 0)
    spans = jnp.where(row < count, 2 * (here[0] - 1 - row), 2 * here[0]) + here[1]
    weight = jnp.exp((jnp.maximum(spans, 0) * hours).astype(F32) * rate)
    weight = jnp.where((row < here[0]) | (row == count), weight, 0.0)
    weight = jnp.where(row == count, weight * initial[...], weight)
    chain[...] = jnp.where(row == count + 1, here[1].astype(F32), weight)
    block = column(hour_block[...], hours)
    blocks = block_price.shape[1]
    price = jnp.where(block == iota((hours, blocks), 1), block_price[...], 0.0)
    hour_price[...] = jnp.broadcast_to(jnp.sum(price, axis=1, keepdims=True), hour_price.shape)


def clipped(flows, dual, limit):
    shifted = flows + dual
    return shifted - jnp.clip(shifted, -limit, limit)


def pull_parts(dual, ptdf, out):
    pull = jnp.dot(dual.astype(BF16), ptdf[...], preferred_element_type=F32)
    rows = out.shape[2]
    for d in range(out.shape[0]):
        out[d] = pull[:, d * rows : (d + 1) * rows].astype(BF16)


def first_body(
    chip, core, arrived, ptdf,
    bus_in, dual_in, rating_in, index_in, leakage_in, block_in, prices_in, initial_in,
    parts, dual_out, unit_flow_out, row_sum, limit, growth, hour_price, chain, held,
    bus, line_dual, rating, index, leakage, hour_block, block_price, initial,
    lefts, owned, hot, small_sems, sems
):
    here = chip[0], core[0]
    sources = (bus_in, dual_in, rating_in, index_in, leakage_in, block_in, prices_in, initial_in)
    targets = (bus, line_dual, rating, index, leakage, hour_block, block_price, initial)
    small = [
        pltpu.make_async_copy(a, b, small_sems.at[k])
        for k, (a, b) in enumerate(zip(sources, targets))
    ]
    for copy in small:
        copy.start()
    chunk = held.shape[0] // CHUNKS
    spans = [pl.ds(k * chunk, chunk) for k in range(CHUNKS)]
    copies = [
        pltpu.make_async_copy(ptdf.at[at], held.at[at], sems.at[k]) for k, at in enumerate(spans)
    ]
    for copy in copies:
        copy.start()
    count, hours, width = arrived.shape
    rows = parts.shape[2]
    units = width - rows
    for d in range(count):
        at = slice(d * rows, (d + 1) * rows)
        lefts[:hours, at] = arrived[d, :, :rows]
        lefts[3 * hours :, at] = (iota((count, rows), 0) == d).astype(F32).astype(BF16)
    for copy in small:
        copy.wait()
    write_tables(
        here, rating, index, leakage, hour_block, block_price, initial, limit, growth, hour_price, chain
    )
    owner, place = bus[...] // rows, bus[...] % rows
    bus_row = iota((rows, units), 0)
    for k in range(count):
        at = slice(k * units, (k + 1) * units)
        hot[:, at] = (bus_row == place[:, at]).astype(F32).astype(BF16)
        for d in range(count):
            mine = jnp.broadcast_to((owner[:, at] == d).astype(F32), (16, units)).astype(BF16)
            for h in range(0, hours, 16):
                owned[d * hours + h : d * hours + h + 16, at] = arrived[k, h : h + 16, rows:] * mine
    spread = lax.dot_general(owned[...], hot[...], NT, preferred_element_type=F32)
    for d in range(count):
        part = spread[d * hours : (d + 1) * hours]
        high = part.astype(BF16)
        at = slice(d * rows, (d + 1) * rows)
        lefts[hours : 2 * hours, at] = high
        lefts[2 * hours : 3 * hours, at] = (part - high.astype(F32)).astype(BF16)
    for copy, at in zip(copies, spans):
        copy.wait()
        products = lax.dot_general(lefts[...], held[at], NT, preferred_element_type=F32)
        unit_flow = products[hours : 2 * hours] + products[2 * hours : 3 * hours]
        row_sum[:, at] = products[3 * hours :]
        unit_flow_out[:, at] = unit_flow
        dual_out[:, at] = clipped(products[:hours] + unit_flow, line_dual[:, at], limit[:, at])
    pull_parts(dual_out[...], held, parts)


def second_body(arrived, ptdf, line_dual, limit, unit_flow, row_sum, parts, dual_out, mean_out):
    count, hours, rows = parts.shape
    notes = jnp.concatenate([arrived[d, hours : hours + 8] for d in range(count)], axis=0)
    notes = notes.astype(F32)
    notes = notes[:, :hours] + notes[:, hours : 2 * hours] + notes[:, 2 * hours : 3 * hours]
    means = jnp.concatenate([notes[8 * d : 8 * d + 1] for d in range(count)], axis=0)
    units = jnp.concatenate([notes[8 * d + 1 : 8 * d + 2] for d in range(count)], axis=0)
    mean = jnp.sum(means * rows + units, axis=0, keepdims=True) / (count * rows)
    mean_out[...] = jnp.broadcast_to(column(mean, hours), mean_out.shape)
    balance = jnp.concatenate([arrived[d, :hours] for d in range(count)], axis=1)
    flows = lax.dot_general(balance, ptdf[...], NT, preferred_element_type=F32)
    flows += lax.dot_general(
        means - mean,
        row_sum[...],
        (((0,), (0,)), ((), ())),
        precision=lax.Precision.HIGHEST,
        preferred_element_type=F32,
    )
    dual = clipped(flows + unit_flow[...], line_dual[...], limit[...])
    dual_out[...] = dual
    pull_parts(dual, ptdf, parts)


def note(col, width):
    n = col.shape[0]
    high, middle, low = (part.astype(F32) for part in three_parts(col))
    lane = iota((n, width), 1)
    value = jnp.where(lane < n, high, jnp.where(lane < 2 * n, middle, low))
    mine = (lane % n == iota((n, width), 0)) & (lane < 3 * n)
    return jnp.sum(jnp.where(mine, value, 0.0), axis=0, keepdims=True)


def total_of(arrived):
    total = arrived[0].astype(F32)
    for d in range(1, arrived.shape[0]):
        total += arrived[d].astype(F32)
    return total


def trial_body(arrived, gen, cost, demand, price, cap, storage, send, trial_out):
    hours = gen.shape[0]
    pull = total_of(arrived)
    now = column(price[...], hours)
    trial = jnp.clip(gen[...] - STEP * (cost[...] - now + pull), 0.0, cap[...])
    trial_out[...] = trial
    balance = trial - demand[...]
    width = balance.shape[1]
    mean = jnp.sum(balance, axis=1, keepdims=True) / width
    unit_sum = jnp.sum(storage[...], axis=1, keepdims=True)
    row = iota((8, width), 0)
    below = jnp.where(row == 0, note(mean, width), jnp.where(row == 1, note(unit_sum, width), 0.0))
    below = below.astype(BF16)
    around = (balance - mean).astype(BF16)
    for d in range(send.shape[0]):
        send[d, :hours] = around
        send[d, hours:] = below


def last_trial_body(arrived, before, mean, cost, demand, price, cap, storage, send, trial_out):
    hours = before.shape[0]
    pull = total_of(arrived)
    moved = mean[:, :1]
    now = column(price[...], hours) - BAL * moved
    trial = jnp.clip(before[...] - moved - STEP * (cost[...] - now + pull), 0.0, cap[...])
    trial_out[...] = trial
    own = jnp.sum(trial - demand[...], axis=1, keepdims=True)
    own += jnp.sum(storage[...], axis=1, keepdims=True)
    send[...] = jnp.broadcast_to(row_of(own, send.shape[2])[None], send.shape)


def finish_body(
    arrived, trial, mean, price, hour_price, storage, wear, growth, gen_out, storage_out, running_out, price_out, last_out
):
    hours, units = storage.shape
    buses = arrived.shape[0] * trial.shape[1]
    mismatch = column(total_of(arrived)[:1], hours) / buses
    gen_out[...] = trial[...] - mismatch
    now = column(price[...], hours) - BAL * mean[:, :1] - BAL * mismatch
    price_out[...] = row_of(now, price_out.shape[1])
    held = storage[...]
    nexts = jnp.clip(held + STEP_UNIT * (now + hour_price[...] - wear[...] * held), -1.0, 1.0)
    storage_out[...] = nexts
    running = -ETA * nexts
    hour = iota((hours, units), 0)
    span = 1
    while span < hours:
        moved = jnp.where(hour >= span, pltpu.roll(running, span, 0), 0.0)
        running = running + growth[span - 1 : span] * moved
        span *= 2
    running_out[...] = running
    last_out[...] = jnp.broadcast_to(running[hours - 1 :], last_out.shape)


def chip_body(pair, growth, send):
    hours = growth.shape[0]
    both = growth[hours - 1 :] * pair[0] + pair[1]
    send[...] = jnp.broadcast_to(both[None], send.shape)


def charge_body(arrived, pair, growth, chain, running, charge):
    count = arrived.shape[0]
    entering = chain[count : count + 1] + chain[count + 1 : count + 2] * pair[0, :1]
    for k in range(count):
        entering += chain[k : k + 1] * arrived[k, :1]
    charge[...] = growth[...] * entering + running[...]


def in_hbm(array):
    return pltpu.with_memory_space_constraint(array, pltpu.HBM)


def everywhere(blocks, axis):
    return lax.all_to_all(blocks, axis, split_axis=0, concat_axis=0, tiled=True)


def per_device(
    ptdf,
    demand,
    generation,
    cost,
    gen_cap,
    storage,
    wear,
    initial_charge,
    leakage,
    line_dual,
    line_index,
    rating,
    storage_bus,
    balance_dual,
    hour_block,
    block_price,
):
    net = lax.axis_size("net")
    chips = lax.axis_size("tm_0")
    lines = ptdf.shape[0]
    rows, hours = generation.shape
    units = storage.shape[0]
    demand, gen, cost, held = demand.T, generation.T, cost.T, storage.T
    dual = line_dual.T
    cap, wear, initial = gen_cap[None], wear[None], initial_charge[None]
    price = balance_dual[None]
    chip, core, gen = lax.optimization_barrier(
        (lax.axis_index("tm_0").reshape(1), lax.axis_index("tm_1").reshape(1), gen)
    )
    packed = pl.pallas_call(
        pack_body,
        name="pack",
        in_specs=[pl.BlockSpec(memory_space=pltpu.HBM)] * 3,
        out_shape=jax.ShapeDtypeStruct((net, hours, rows + units), BF16),
        scratch_shapes=[
            pltpu.VMEM((hours, rows), F32),
            pltpu.VMEM((hours, rows), F32),
            pltpu.VMEM((hours, units), F32),
            pltpu.SemaphoreType.DMA((3,)),
        ],
        compiler_params=pltpu.CompilerParams(vmem_limit_bytes=VMEM_LIMIT),
    )(*(in_hbm(a) for a in (gen, demand, held)))
    arrived = everywhere(packed, "net")
    sources = (
        storage_bus[None],
        dual,
        rating.reshape(-1, 128),
        line_index[None],
        leakage[None],
        hour_block[None],
        block_price[None],
        initial,
    )
    smem, hbm = (pl.BlockSpec(memory_space=m) for m in (pltpu.SMEM, pltpu.HBM))
    parts, dual, unit_flow, row_sum, limit, growth, hour_price, chain, kept = pl.pallas_call(
        first_body,
        name="first",
        in_specs=[smem, smem, pl.BlockSpec(), hbm] + [hbm] * len(sources),
        out_shape=(
            jax.ShapeDtypeStruct((net, hours, rows), BF16),
            jax.ShapeDtypeStruct((hours, lines), F32),
            jax.ShapeDtypeStruct((hours, lines), F32),
            jax.ShapeDtypeStruct((net, lines), F32),
            jax.ShapeDtypeStruct((1, lines), F32),
            jax.ShapeDtypeStruct((hours, units), F32),
            jax.ShapeDtypeStruct((hours, units), F32),
            jax.ShapeDtypeStruct((chips + 8, units), F32),
            jax.ShapeDtypeStruct(ptdf.shape, BF16),
        ),
        scratch_shapes=[
            *(pltpu.VMEM(a.shape, a.dtype) for a in sources),
            pltpu.VMEM((3 * hours + net, net * rows), BF16),
            pltpu.VMEM((net * hours, net * units), BF16),
            pltpu.VMEM((rows, net * units), BF16),
            pltpu.SemaphoreType.DMA((len(sources),)),
            pltpu.SemaphoreType.DMA((CHUNKS,)),
        ],
        compiler_params=pltpu.CompilerParams(vmem_limit_bytes=VMEM_LIMIT),
    )(chip, core, arrived, *(in_hbm(a) for a in (ptdf, *sources)))
    arrived = everywhere(parts, "net")
    send, trial = call(
        trial_body, "trial", shape((net, hours + 8, rows), BF16), shape((hours, rows), F32)
    )(arrived, gen, cost, demand, price, cap, held)
    arrived = everywhere(send, "net")
    parts, dual, mean = call(
        second_body,
        "second",
        shape((net, hours, rows), BF16),
        shape((hours, lines), F32),
        shape((hours, 128), F32),
    )(arrived, kept, dual, limit, unit_flow, row_sum)
    arrived = everywhere(parts, "net")
    send, trial = call(
        last_trial_body, "last_trial", shape((net, 8, 128), F32), shape((hours, rows), F32)
    )(arrived, trial, mean, cost, demand, price, cap, held)
    arrived = everywhere(send, "net")
    gen, storage_next, running, price, last = call(
        finish_body,
        "finish",
        shape((hours, rows), F32),
        shape((hours, units), F32),
        shape((hours, units), F32),
        shape((1, hours), F32),
        shape((8, units), F32),
    )(arrived, trial, mean, price, hour_price, held, wear, growth)
    pair = lax.all_gather(last, "tm_1")
    (send,) = call(chip_body, "chip", shape((chips, 8, units), F32))(pair, growth)
    arrived = everywhere(send, "tm_0")
    (charge,) = call(charge_body, "charge", shape((hours, units), F32))(
        arrived, pair, growth, chain, running
    )
    return (gen.T, storage_next.T, charge.T, dual.T, price[0])


def solution(mesh):
    split = Mesh(mesh.devices.reshape(16, 2, mesh.shape["net"]), ("tm_0", "tm_1", "net"))
    in_specs = (
        P("net", None),
        P("net", TM),
        P("net", TM),
        P("net", TM),
        P("net"),
        P("net", TM),
        P("net"),
        P("net"),
        P("net"),
        P("net", TM),
        P("net"),
        P(),
        P(),
        P(TM),
        P(TM),
        P(),
    )
    out_specs = (P("net", TM), P("net", TM), P("net", TM), P("net", TM), P(TM))
    return jax.shard_map(
        per_device, mesh=split, in_specs=in_specs, out_specs=out_specs, check_vma=False
    )
```

```python
import jax
import jax.numpy as jnp
from jax import lax
from jax.experimental import pallas as pl
from jax.experimental.pallas import tpu as pltpu
from jax.sharding import Mesh
from jax.sharding import PartitionSpec as P

TM = ("tm_0", "tm_1")

STEP = 0.1
BAL = 0.5
STEP_UNIT = 0.2
ETA = 0.0625

F32 = jnp.float32
VMEM_LIMIT = 16 << 20
BF16 = jnp.bfloat16
NT = (((1,), (1,)), ((), ()))


def call(kernel, name, *outs):
    return pl.pallas_call(
        kernel,
        name=name,
        out_shape=tuple(jax.ShapeDtypeStruct(s, d) for s, d in outs),
        compiler_params=pltpu.CompilerParams(vmem_limit_bytes=VMEM_LIMIT),
    )


def shape(s, d):
    return s, d


def iota(dims, axis):
    return lax.broadcasted_iota(jnp.int32, dims, axis)


def column(row, n):
    eye = iota((n, n), 0) == iota((n, n), 1)
    return jnp.sum(jnp.where(eye, row[:, :n], jnp.zeros((), row.dtype)), axis=1, keepdims=True)


def row_of(col, width):
    n = col.shape[0]
    eye = iota((n, width), 0) == iota((n, width), 1)
    return jnp.sum(jnp.where(eye, col, 0.0), axis=0, keepdims=True)


def three_parts(value):
    high = value.astype(BF16)
    rest = value - high.astype(F32)
    middle = rest.astype(BF16)
    low = (rest - middle.astype(F32)).astype(BF16)
    return high, middle, low


def pack_body(
    chip, core, gen_in, demand_in, storage_in, bus_in, dual_in, rating_in, index_in, leakage_in,
    block_in, prices_in, initial_in,
    out, limit, growth, hour_price, chain, bus, line_dual,
    gen, demand, storage, rating, index, leakage, hour_block, block_price, initial, sems
):
    pairs = (
        (gen_in, gen),
        (demand_in, demand),
        (storage_in, storage),
        (rating_in, rating),
        (index_in, index),
        (leakage_in, leakage),
        (block_in, hour_block),
        (prices_in, block_price),
        (initial_in, initial),
        (bus_in, bus),
        (dual_in, line_dual),
    )
    copies = [pltpu.make_async_copy(a, b, sems.at[k]) for k, (a, b) in enumerate(pairs)]
    for copy in copies:
        copy.start()
    for copy in copies:
        copy.wait()
    here = chip[0], core[0]
    write_tables(
        here, rating, index, leakage, hour_block, block_price, initial, limit, growth, hour_price, chain
    )
    rows = gen.shape[1]
    injection = (gen[...] - demand[...]).astype(BF16)
    units = storage[...].astype(BF16)
    for d in range(out.shape[0]):
        out[d, :, :rows] = injection
        out[d, :, rows:] = units


def write_tables(
    here, rating, index, leakage, hour_block, block_price, initial, limit, growth, hour_price, chain
):
    groups = rating.shape[0]
    at = index[...]
    hot = (iota((groups, at.shape[1]), 0) == at // 128).astype(BF16)
    table = rating[...].T
    picked = sum(jnp.dot(part, hot, preferred_element_type=F32) for part in three_parts(table))
    found = iota((128, at.shape[1]), 0) == at % 128
    limit[...] = jnp.sum(jnp.where(found, picked, 0.0), axis=0, keepdims=True)
    hours, units = growth.shape
    offsets = (iota((hours, units), 0) + 1).astype(F32)
    rate = jnp.log(1.0 - leakage[...])
    growth[...] = jnp.exp(offsets * rate)
    count = chain.shape[0] - 8
    row = iota(chain.shape, 0)
    spans = jnp.where(row < count, 2 * (here[0] - 1 - row), 2 * here[0]) + here[1]
    weight = jnp.exp((jnp.maximum(spans, 0) * hours).astype(F32) * rate)
    weight = jnp.where((row < here[0]) | (row == count), weight, 0.0)
    weight = jnp.where(row == count, weight * initial[...], weight)
    chain[...] = jnp.where(row == count + 1, here[1].astype(F32), weight)
    block = column(hour_block[...], hours)
    blocks = block_price.shape[1]
    price = jnp.where(block == iota((hours, blocks), 1), block_price[...], 0.0)
    hour_price[...] = jnp.broadcast_to(jnp.sum(price, axis=1, keepdims=True), hour_price.shape)


def clipped(flows, dual, limit):
    shifted = flows + dual
    return shifted - jnp.clip(shifted, -limit, limit)


def pull_parts(dual, ptdf, out):
    pull = jnp.dot(dual.astype(BF16), ptdf[...], preferred_element_type=F32)
    rows = out.shape[2]
    for d in range(out.shape[0]):
        out[d] = pull[:, d * rows : (d + 1) * rows].astype(BF16)


def first_body(
    arrived, ptdf, bus, line_dual, limit, parts, dual_out, unit_flow_out, row_sum, held,
    lefts, owned, hot, sem
):
    copy = pltpu.make_async_copy(ptdf, held, sem)
    copy.start()
    count, hours, width = arrived.shape
    rows = parts.shape[2]
    units = width - rows
    for d in range(count):
        at = slice(d * rows, (d + 1) * rows)
        lefts[:hours, at] = arrived[d, :, :rows]
        lefts[3 * hours :, at] = (iota((count, rows), 0) == d).astype(F32).astype(BF16)
    owner, place = bus[...] // rows, bus[...] % rows
    bus_row = iota((rows, units), 0)
    for k in range(count):
        at = slice(k * units, (k + 1) * units)
        hot[:, at] = (bus_row == place[:, at]).astype(F32).astype(BF16)
        for d in range(count):
            mine = jnp.broadcast_to((owner[:, at] == d).astype(F32), (16, units)).astype(BF16)
            for h in range(0, hours, 16):
                owned[d * hours + h : d * hours + h + 16, at] = arrived[k, h : h + 16, rows:] * mine
    spread = lax.dot_general(owned[...], hot[...], NT, preferred_element_type=F32)
    for d in range(count):
        part = spread[d * hours : (d + 1) * hours]
        high = part.astype(BF16)
        at = slice(d * rows, (d + 1) * rows)
        lefts[hours : 2 * hours, at] = high
        lefts[2 * hours : 3 * hours, at] = (part - high.astype(F32)).astype(BF16)
    copy.wait()
    products = lax.dot_general(lefts[...], held[...], NT, preferred_element_type=F32)
    unit_flow = products[hours : 2 * hours] + products[2 * hours : 3 * hours]
    row_sum[...] = products[3 * hours :]
    unit_flow_out[...] = unit_flow
    dual = clipped(products[:hours] + unit_flow, line_dual[...], limit[...])
    dual_out[...] = dual
    pull_parts(dual, held, parts)


def second_body(arrived, ptdf, line_dual, limit, unit_flow, row_sum, parts, dual_out, mean_out):
    count, hours, rows = parts.shape
    notes = jnp.concatenate([arrived[d, hours : hours + 8] for d in range(count)], axis=0)
    notes = notes.astype(F32)
    notes = notes[:, :hours] + notes[:, hours : 2 * hours] + notes[:, 2 * hours : 3 * hours]
    means = jnp.concatenate([notes[8 * d : 8 * d + 1] for d in range(count)], axis=0)
    units = jnp.concatenate([notes[8 * d + 1 : 8 * d + 2] for d in range(count)], axis=0)
    mean = jnp.sum(means * rows + units, axis=0, keepdims=True) / (count * rows)
    mean_out[...] = jnp.broadcast_to(column(mean, hours), mean_out.shape)
    balance = jnp.concatenate([arrived[d, :hours] for d in range(count)], axis=1)
    flows = lax.dot_general(balance, ptdf[...], NT, preferred_element_type=F32)
    flows += lax.dot_general(
        means - mean,
        row_sum[...],
        (((0,), (0,)), ((), ())),
        precision=lax.Precision.HIGHEST,
        preferred_element_type=F32,
    )
    dual = clipped(flows + unit_flow[...], line_dual[...], limit[...])
    dual_out[...] = dual
    pull_parts(dual, ptdf, parts)


def note(col, width):
    n = col.shape[0]
    high, middle, low = (part.astype(F32) for part in three_parts(col))
    lane = iota((n, width), 1)
    value = jnp.where(lane < n, high, jnp.where(lane < 2 * n, middle, low))
    mine = (lane % n == iota((n, width), 0)) & (lane < 3 * n)
    return jnp.sum(jnp.where(mine, value, 0.0), axis=0, keepdims=True)


def total_of(arrived):
    total = arrived[0].astype(F32)
    for d in range(1, arrived.shape[0]):
        total += arrived[d].astype(F32)
    return total


def trial_body(arrived, gen, cost, demand, price, cap, storage, send, trial_out):
    hours = gen.shape[0]
    pull = total_of(arrived)
    now = column(price[...], hours)
    trial = jnp.clip(gen[...] - STEP * (cost[...] - now + pull), 0.0, cap[...])
    trial_out[...] = trial
    balance = trial - demand[...]
    width = balance.shape[1]
    mean = jnp.sum(balance, axis=1, keepdims=True) / width
    unit_sum = jnp.sum(storage[...], axis=1, keepdims=True)
    row = iota((8, width), 0)
    below = jnp.where(row == 0, note(mean, width), jnp.where(row == 1, note(unit_sum, width), 0.0))
    below = below.astype(BF16)
    around = (balance - mean).astype(BF16)
    for d in range(send.shape[0]):
        send[d, :hours] = around
        send[d, hours:] = below


def last_trial_body(arrived, before, mean, cost, demand, price, cap, storage, send, trial_out):
    hours = before.shape[0]
    pull = total_of(arrived)
    moved = mean[:, :1]
    now = column(price[...], hours) - BAL * moved
    trial = jnp.clip(before[...] - moved - STEP * (cost[...] - now + pull), 0.0, cap[...])
    trial_out[...] = trial
    own = jnp.sum(trial - demand[...], axis=1, keepdims=True)
    own += jnp.sum(storage[...], axis=1, keepdims=True)
    send[...] = jnp.broadcast_to(row_of(own, send.shape[2])[None], send.shape)


def finish_body(
    arrived, trial, mean, price, hour_price, storage, wear, growth, gen_out, storage_out, running_out, price_out, last_out
):
    hours, units = storage.shape
    buses = arrived.shape[0] * trial.shape[1]
    mismatch = column(total_of(arrived)[:1], hours) / buses
    gen_out[...] = trial[...] - mismatch
    now = column(price[...], hours) - BAL * mean[:, :1] - BAL * mismatch
    price_out[...] = row_of(now, price_out.shape[1])
    held = storage[...]
    nexts = jnp.clip(held + STEP_UNIT * (now + hour_price[...] - wear[...] * held), -1.0, 1.0)
    storage_out[...] = nexts
    running = -ETA * nexts
    hour = iota((hours, units), 0)
    span = 1
    while span < hours:
        moved = jnp.where(hour >= span, pltpu.roll(running, span, 0), 0.0)
        running = running + growth[span - 1 : span] * moved
        span *= 2
    running_out[...] = running
    last_out[...] = jnp.broadcast_to(running[hours - 1 :], last_out.shape)


def chip_body(pair, growth, send):
    hours = growth.shape[0]
    both = growth[hours - 1 :] * pair[0] + pair[1]
    send[...] = jnp.broadcast_to(both[None], send.shape)


def charge_body(arrived, pair, growth, chain, running, charge):
    count = arrived.shape[0]
    entering = chain[count : count + 1] + chain[count + 1 : count + 2] * pair[0, :1]
    for k in range(count):
        entering += chain[k : k + 1] * arrived[k, :1]
    charge[...] = growth[...] * entering + running[...]


def in_hbm(array):
    return pltpu.with_memory_space_constraint(array, pltpu.HBM)


def everywhere(blocks, axis):
    return lax.all_to_all(blocks, axis, split_axis=0, concat_axis=0, tiled=True)


def per_device(
    ptdf,
    demand,
    generation,
    cost,
    gen_cap,
    storage,
    wear,
    initial_charge,
    leakage,
    line_dual,
    line_index,
    rating,
    storage_bus,
    balance_dual,
    hour_block,
    block_price,
):
    net = lax.axis_size("net")
    chips = lax.axis_size("tm_0")
    lines = ptdf.shape[0]
    rows, hours = generation.shape
    units = storage.shape[0]
    demand, gen, cost, held = demand.T, generation.T, cost.T, storage.T
    dual = line_dual.T
    cap, wear, initial = gen_cap[None], wear[None], initial_charge[None]
    price = balance_dual[None]
    chip, core, gen = lax.optimization_barrier(
        (lax.axis_index("tm_0").reshape(1), lax.axis_index("tm_1").reshape(1), gen)
    )
    sources = (
        gen,
        demand,
        held,
        storage_bus[None],
        dual,
        rating.reshape(-1, 128),
        line_index[None],
        leakage[None],
        hour_block[None],
        block_price[None],
        initial,
    )
    smem, hbm = (pl.BlockSpec(memory_space=m) for m in (pltpu.SMEM, pltpu.HBM))
    packed, limit, growth, hour_price, chain, bus, dual = pl.pallas_call(
        pack_body,
        name="pack",
        in_specs=[smem, smem] + [hbm] * len(sources),
        out_shape=(
            jax.ShapeDtypeStruct((net, hours, rows + units), BF16),
            jax.ShapeDtypeStruct((1, lines), F32),
            jax.ShapeDtypeStruct((hours, units), F32),
            jax.ShapeDtypeStruct((hours, units), F32),
            jax.ShapeDtypeStruct((chips + 8, units), F32),
            jax.ShapeDtypeStruct((1, net * units), jnp.int32),
            jax.ShapeDtypeStruct((hours, lines), F32),
        ),
        scratch_shapes=[
            *(pltpu.VMEM(a.shape, a.dtype) for a in sources[:3] + sources[5:]),
            pltpu.SemaphoreType.DMA((len(sources),)),
        ],
        compiler_params=pltpu.CompilerParams(vmem_limit_bytes=VMEM_LIMIT),
    )(chip, core, *(in_hbm(a) for a in sources))
    arrived = everywhere(packed, "net")
    parts, dual, unit_flow, row_sum, ptdf = pl.pallas_call(
        first_body,
        name="first",
        in_specs=[pl.BlockSpec(), hbm] + [pl.BlockSpec()] * 3,
        out_shape=(
            jax.ShapeDtypeStruct((net, hours, rows), BF16),
            jax.ShapeDtypeStruct((hours, lines), F32),
            jax.ShapeDtypeStruct((hours, lines), F32),
            jax.ShapeDtypeStruct((net, lines), F32),
            jax.ShapeDtypeStruct(ptdf.shape, BF16),
        ),
        scratch_shapes=[
            pltpu.VMEM((3 * hours + net, net * rows), BF16),
            pltpu.VMEM((net * hours, net * units), BF16),
            pltpu.VMEM((rows, net * units), BF16),
            pltpu.SemaphoreType.DMA(()),
        ],
        compiler_params=pltpu.CompilerParams(vmem_limit_bytes=VMEM_LIMIT),
    )(arrived, in_hbm(ptdf), bus, dual, limit)
    arrived = everywhere(parts, "net")
    send, trial = call(
        trial_body, "trial", shape((net, hours + 8, rows), BF16), shape((hours, rows), F32)
    )(arrived, gen, cost, demand, price, cap, held)
    arrived = everywhere(send, "net")
    parts, dual, mean = call(
        second_body,
        "second",
        shape((net, hours, rows), BF16),
        shape((hours, lines), F32),
        shape((hours, 128), F32),
    )(arrived, ptdf, dual, limit, unit_flow, row_sum)
    arrived = everywhere(parts, "net")
    send, trial = call(
        last_trial_body, "last_trial", shape((net, 8, 128), F32), shape((hours, rows), F32)
    )(arrived, trial, mean, cost, demand, price, cap, held)
    arrived = everywhere(send, "net")
    gen, storage_next, running, price, last = call(
        finish_body,
        "finish",
        shape((hours, rows), F32),
        shape((hours, units), F32),
        shape((hours, units), F32),
        shape((1, hours), F32),
        shape((8, units), F32),
    )(arrived, trial, mean, price, hour_price, held, wear, growth)
    pair = lax.all_gather(last, "tm_1")
    (send,) = call(chip_body, "chip", shape((chips, 8, units), F32))(pair, growth)
    arrived = everywhere(send, "tm_0")
    (charge,) = call(charge_body, "charge", shape((hours, units), F32))(
        arrived, pair, growth, chain, running
    )
    return (gen.T, storage_next.T, charge.T, dual.T, price[0])


def solution(mesh):
    split = Mesh(mesh.devices.reshape(16, 2, mesh.shape["net"]), ("tm_0", "tm_1", "net"))
    in_specs = (
        P("net", None),
        P("net", TM),
        P("net", TM),
        P("net", TM),
        P("net"),
        P("net", TM),
        P("net"),
        P("net"),
        P("net"),
        P("net", TM),
        P("net"),
        P(),
        P(),
        P(TM),
        P(TM),
        P(),
    )
    out_specs = (P("net", TM), P("net", TM), P("net", TM), P("net", TM), P(TM))
    return jax.shard_map(
        per_device, mesh=split, in_specs=in_specs, out_specs=out_specs, check_vma=False
    )
```

```python
import jax
import jax.numpy as jnp
from jax import lax
from jax.experimental import pallas as pl
from jax.experimental.pallas import tpu as pltpu
from jax.sharding import Mesh
from jax.sharding import PartitionSpec as P

TM = ("tm_0", "tm_1")

STEP = 0.1
BAL = 0.5
STEP_UNIT = 0.2
ETA = 0.0625

F32 = jnp.float32
VMEM_LIMIT = 16 << 20
EARLY = 6
BF16 = jnp.bfloat16
NT = (((1,), (1,)), ((), ()))


def call(kernel, name, *outs):
    return pl.pallas_call(
        kernel,
        name=name,
        out_shape=tuple(jax.ShapeDtypeStruct(s, d) for s, d in outs),
        compiler_params=pltpu.CompilerParams(vmem_limit_bytes=VMEM_LIMIT),
    )


def shape(s, d):
    return s, d


def iota(dims, axis):
    return lax.broadcasted_iota(jnp.int32, dims, axis)


def column(row, n):
    eye = iota((n, n), 0) == iota((n, n), 1)
    return jnp.sum(jnp.where(eye, row[:, :n], jnp.zeros((), row.dtype)), axis=1, keepdims=True)


def row_of(col, width):
    n = col.shape[0]
    eye = iota((n, width), 0) == iota((n, width), 1)
    return jnp.sum(jnp.where(eye, col, 0.0), axis=0, keepdims=True)


def three_parts(value):
    high = value.astype(BF16)
    rest = value - high.astype(F32)
    middle = rest.astype(BF16)
    low = (rest - middle.astype(F32)).astype(BF16)
    return high, middle, low


def pack_body(
    chip, core, gen_in, demand_in, storage_in, bus_in, dual_in, rating_in, index_in, leakage_in,
    block_in, prices_in, initial_in, ptdf,
    out, limit, growth, hour_price, chain, bus, line_dual, begun,
    gen, demand, storage, rating, index, leakage, hour_block, block_price, initial, sems
):
    pairs = (
        (gen_in, gen),
        (demand_in, demand),
        (storage_in, storage),
        (rating_in, rating),
        (index_in, index),
        (leakage_in, leakage),
        (block_in, hour_block),
        (prices_in, block_price),
        (initial_in, initial),
        (bus_in, bus),
        (dual_in, line_dual),
    )
    copies = [pltpu.make_async_copy(a, b, sems.at[k]) for k, (a, b) in enumerate(pairs)]
    for copy in copies:
        copy.start()
    first_rows = pl.ds(0, begun.shape[0] * EARLY // 16)
    early = pltpu.make_async_copy(ptdf.at[first_rows], begun.at[first_rows], sems.at[len(pairs)])
    early.start()
    for copy in copies[:3]:
        copy.wait()
    rows = gen.shape[1]
    injection = (gen[...] - demand[...]).astype(BF16)
    units = storage[...].astype(BF16)
    for d in range(out.shape[0]):
        out[d, :, :rows] = injection
        out[d, :, rows:] = units
    for copy in copies[3:]:
        copy.wait()
    here = chip[0], core[0]
    write_tables(
        here, rating, index, leakage, hour_block, block_price, initial, limit, growth, hour_price, chain
    )
    early.wait()


def write_tables(
    here, rating, index, leakage, hour_block, block_price, initial, limit, growth, hour_price, chain
):
    groups = rating.shape[0]
    at = index[...]
    hot = (iota((groups, at.shape[1]), 0) == at // 128).astype(BF16)
    table = rating[...].T
    picked = sum(jnp.dot(part, hot, preferred_element_type=F32) for part in three_parts(table))
    found = iota((128, at.shape[1]), 0) == at % 128
    limit[...] = jnp.sum(jnp.where(found, picked, 0.0), axis=0, keepdims=True)
    hours, units = growth.shape
    offsets = (iota((hours, units), 0) + 1).astype(F32)
    rate = jnp.log(1.0 - leakage[...])
    growth[...] = jnp.exp(offsets * rate)
    count = chain.shape[0] - 8
    row = iota(chain.shape, 0)
    spans = jnp.where(row < count, 2 * (here[0] - 1 - row), 2 * here[0]) + here[1]
    weight = jnp.exp((jnp.maximum(spans, 0) * hours).astype(F32) * rate)
    weight = jnp.where((row < here[0]) | (row == count), weight, 0.0)
    weight = jnp.where(row == count, weight * initial[...], weight)
    chain[...] = jnp.where(row == count + 1, here[1].astype(F32), weight)
    block = column(hour_block[...], hours)
    blocks = block_price.shape[1]
    price = jnp.where(block == iota((hours, blocks), 1), block_price[...], 0.0)
    hour_price[...] = jnp.broadcast_to(jnp.sum(price, axis=1, keepdims=True), hour_price.shape)


def clipped(flows, dual, limit):
    shifted = flows + dual
    return shifted - jnp.clip(shifted, -limit, limit)


def pull_parts(dual, ptdf, out):
    pull = jnp.dot(dual.astype(BF16), ptdf[...], preferred_element_type=F32)
    rows = out.shape[2]
    for d in range(out.shape[0]):
        out[d] = pull[:, d * rows : (d + 1) * rows].astype(BF16)


def first_body(
    arrived, ptdf, bus, line_dual, limit, begun, parts, dual_out, unit_flow_out, row_sum, held,
    lefts, owned, hot, sem
):
    early = held.shape[0] * EARLY // 16
    rest = pl.ds(early, held.shape[0] - early)
    copy = pltpu.make_async_copy(ptdf.at[rest], held.at[rest], sem)
    copy.start()
    count, hours, width = arrived.shape
    rows = parts.shape[2]
    units = width - rows
    for d in range(count):
        at = slice(d * rows, (d + 1) * rows)
        lefts[:hours, at] = arrived[d, :, :rows]
        lefts[3 * hours :, at] = (iota((count, rows), 0) == d).astype(F32).astype(BF16)
    owner, place = bus[...] // rows, bus[...] % rows
    bus_row = iota((rows, units), 0)
    for k in range(count):
        at = slice(k * units, (k + 1) * units)
        hot[:, at] = (bus_row == place[:, at]).astype(F32).astype(BF16)
        for d in range(count):
            mine = jnp.broadcast_to((owner[:, at] == d).astype(F32), (16, units)).astype(BF16)
            for h in range(0, hours, 16):
                owned[d * hours + h : d * hours + h + 16, at] = arrived[k, h : h + 16, rows:] * mine
    spread = lax.dot_general(owned[...], hot[...], NT, preferred_element_type=F32)
    for d in range(count):
        part = spread[d * hours : (d + 1) * hours]
        high = part.astype(BF16)
        at = slice(d * rows, (d + 1) * rows)
        lefts[hours : 2 * hours, at] = high
        lefts[2 * hours : 3 * hours, at] = (part - high.astype(F32)).astype(BF16)
    copy.wait()
    products = lax.dot_general(lefts[...], held[...], NT, preferred_element_type=F32)
    unit_flow = products[hours : 2 * hours] + products[2 * hours : 3 * hours]
    row_sum[...] = products[3 * hours :]
    unit_flow_out[...] = unit_flow
    dual = clipped(products[:hours] + unit_flow, line_dual[...], limit[...])
    dual_out[...] = dual
    pull_parts(dual, held, parts)


def second_body(arrived, ptdf, line_dual, limit, unit_flow, row_sum, parts, dual_out, mean_out):
    count, hours, rows = parts.shape
    notes = jnp.concatenate([arrived[d, hours : hours + 8] for d in range(count)], axis=0)
    notes = notes.astype(F32)
    notes = notes[:, :hours] + notes[:, hours : 2 * hours] + notes[:, 2 * hours : 3 * hours]
    means = jnp.concatenate([notes[8 * d : 8 * d + 1] for d in range(count)], axis=0)
    units = jnp.concatenate([notes[8 * d + 1 : 8 * d + 2] for d in range(count)], axis=0)
    mean = jnp.sum(means * rows + units, axis=0, keepdims=True) / (count * rows)
    mean_out[...] = jnp.broadcast_to(column(mean, hours), mean_out.shape)
    balance = jnp.concatenate([arrived[d, :hours] for d in range(count)], axis=1)
    flows = lax.dot_general(balance, ptdf[...], NT, preferred_element_type=F32)
    flows += lax.dot_general(
        means - mean,
        row_sum[...],
        (((0,), (0,)), ((), ())),
        precision=lax.Precision.HIGHEST,
        preferred_element_type=F32,
    )
    dual = clipped(flows + unit_flow[...], line_dual[...], limit[...])
    dual_out[...] = dual
    pull_parts(dual, ptdf, parts)


def note(col, width):
    n = col.shape[0]
    high, middle, low = (part.astype(F32) for part in three_parts(col))
    lane = iota((n, width), 1)
    value = jnp.where(lane < n, high, jnp.where(lane < 2 * n, middle, low))
    mine = (lane % n == iota((n, width), 0)) & (lane < 3 * n)
    return jnp.sum(jnp.where(mine, value, 0.0), axis=0, keepdims=True)


def total_of(arrived):
    total = arrived[0].astype(F32)
    for d in range(1, arrived.shape[0]):
        total += arrived[d].astype(F32)
    return total


def trial_body(arrived, gen, cost, demand, price, cap, storage, send, trial_out):
    hours = gen.shape[0]
    pull = total_of(arrived)
    now = column(price[...], hours)
    trial = jnp.clip(gen[...] - STEP * (cost[...] - now + pull), 0.0, cap[...])
    trial_out[...] = trial
    balance = trial - demand[...]
    width = balance.shape[1]
    mean = jnp.sum(balance, axis=1, keepdims=True) / width
    unit_sum = jnp.sum(storage[...], axis=1, keepdims=True)
    row = iota((8, width), 0)
    below = jnp.where(row == 0, note(mean, width), jnp.where(row == 1, note(unit_sum, width), 0.0))
    below = below.astype(BF16)
    around = (balance - mean).astype(BF16)
    for d in range(send.shape[0]):
        send[d, :hours] = around
        send[d, hours:] = below


def last_trial_body(arrived, before, mean, cost, demand, price, cap, storage, send, trial_out):
    hours = before.shape[0]
    pull = total_of(arrived)
    moved = mean[:, :1]
    now = column(price[...], hours) - BAL * moved
    trial = jnp.clip(before[...] - moved - STEP * (cost[...] - now + pull), 0.0, cap[...])
    trial_out[...] = trial
    own = jnp.sum(trial - demand[...], axis=1, keepdims=True)
    own += jnp.sum(storage[...], axis=1, keepdims=True)
    send[...] = jnp.broadcast_to(row_of(own, send.shape[2])[None], send.shape)


def finish_body(
    arrived, trial, mean, price, hour_price, storage, wear, growth, gen_out, storage_out, running_out, price_out, last_out
):
    hours, units = storage.shape
    buses = arrived.shape[0] * trial.shape[1]
    mismatch = column(total_of(arrived)[:1], hours) / buses
    gen_out[...] = trial[...] - mismatch
    now = column(price[...], hours) - BAL * mean[:, :1] - BAL * mismatch
    price_out[...] = row_of(now, price_out.shape[1])
    held = storage[...]
    nexts = jnp.clip(held + STEP_UNIT * (now + hour_price[...] - wear[...] * held), -1.0, 1.0)
    storage_out[...] = nexts
    running = -ETA * nexts
    hour = iota((hours, units), 0)
    span = 1
    while span < hours:
        moved = jnp.where(hour >= span, pltpu.roll(running, span, 0), 0.0)
        running = running + growth[span - 1 : span] * moved
        span *= 2
    running_out[...] = running
    last_out[...] = jnp.broadcast_to(running[hours - 1 :], last_out.shape)


def chip_body(pair, growth, send):
    hours = growth.shape[0]
    both = growth[hours - 1 :] * pair[0] + pair[1]
    send[...] = jnp.broadcast_to(both[None], send.shape)


def charge_body(
    arrived, pair, growth, chain, running, gen, storage, dual, price,
    charge_out, gen_out, storage_out, dual_out, price_out, charge, sems
):
    done = ((gen, gen_out), (storage, storage_out), (dual, dual_out), (price, price_out))
    copies = [pltpu.make_async_copy(a, b, sems.at[k]) for k, (a, b) in enumerate(done)]
    for copy in copies:
        copy.start()
    count = arrived.shape[0]
    entering = chain[count : count + 1] + chain[count + 1 : count + 2] * pair[0, :1]
    for k in range(count):
        entering += chain[k : k + 1] * arrived[k, :1]
    charge[...] = growth[...] * entering + running[...]
    last = pltpu.make_async_copy(charge, charge_out, sems.at[len(done)])
    last.start()
    for copy in copies:
        copy.wait()
    last.wait()


def in_hbm(array):
    return pltpu.with_memory_space_constraint(array, pltpu.HBM)


def everywhere(blocks, axis):
    return lax.all_to_all(blocks, axis, split_axis=0, concat_axis=0, tiled=True)


def per_device(
    ptdf,
    demand,
    generation,
    cost,
    gen_cap,
    storage,
    wear,
    initial_charge,
    leakage,
    line_dual,
    line_index,
    rating,
    storage_bus,
    balance_dual,
    hour_block,
    block_price,
):
    net = lax.axis_size("net")
    chips = lax.axis_size("tm_0")
    lines = ptdf.shape[0]
    rows, hours = generation.shape
    units = storage.shape[0]
    demand, gen, cost, held = demand.T, generation.T, cost.T, storage.T
    dual = line_dual.T
    cap, wear, initial = gen_cap[None], wear[None], initial_charge[None]
    price = balance_dual[None]
    chip, core, gen = lax.optimization_barrier(
        (lax.axis_index("tm_0").reshape(1), lax.axis_index("tm_1").reshape(1), gen)
    )
    sources = (
        gen,
        demand,
        held,
        storage_bus[None],
        dual,
        rating.reshape(-1, 128),
        line_index[None],
        leakage[None],
        hour_block[None],
        block_price[None],
        initial,
    )
    smem, hbm = (pl.BlockSpec(memory_space=m) for m in (pltpu.SMEM, pltpu.HBM))
    packed, limit, growth, hour_price, chain, bus, dual, begun = pl.pallas_call(
        pack_body,
        name="pack",
        in_specs=[smem, smem] + [hbm] * (len(sources) + 1),
        out_shape=(
            jax.ShapeDtypeStruct((net, hours, rows + units), BF16),
            jax.ShapeDtypeStruct((1, lines), F32),
            jax.ShapeDtypeStruct((hours, units), F32),
            jax.ShapeDtypeStruct((hours, units), F32),
            jax.ShapeDtypeStruct((chips + 8, units), F32),
            jax.ShapeDtypeStruct((1, net * units), jnp.int32),
            jax.ShapeDtypeStruct((hours, lines), F32),
            jax.ShapeDtypeStruct(ptdf.shape, BF16),
        ),
        scratch_shapes=[
            *(pltpu.VMEM(a.shape, a.dtype) for a in sources[:3] + sources[5:]),
            pltpu.SemaphoreType.DMA((len(sources) + 1,)),
        ],
        compiler_params=pltpu.CompilerParams(vmem_limit_bytes=VMEM_LIMIT),
    )(chip, core, *(in_hbm(a) for a in (*sources, ptdf)))
    arrived = everywhere(packed, "net")
    parts, dual, unit_flow, row_sum, ptdf = pl.pallas_call(
        first_body,
        name="first",
        in_specs=[pl.BlockSpec(), hbm] + [pl.BlockSpec()] * 4,
        input_output_aliases={5: 4},
        out_shape=(
            jax.ShapeDtypeStruct((net, hours, rows), BF16),
            jax.ShapeDtypeStruct((hours, lines), F32),
            jax.ShapeDtypeStruct((hours, lines), F32),
            jax.ShapeDtypeStruct((net, lines), F32),
            jax.ShapeDtypeStruct(ptdf.shape, BF16),
        ),
        scratch_shapes=[
            pltpu.VMEM((3 * hours + net, net * rows), BF16),
            pltpu.VMEM((net * hours, net * units), BF16),
            pltpu.VMEM((rows, net * units), BF16),
            pltpu.SemaphoreType.DMA(()),
        ],
        compiler_params=pltpu.CompilerParams(vmem_limit_bytes=VMEM_LIMIT),
    )(arrived, in_hbm(ptdf), bus, dual, limit, begun)
    arrived = everywhere(parts, "net")
    send, trial = call(
        trial_body, "trial", shape((net, hours + 8, rows), BF16), shape((hours, rows), F32)
    )(arrived, gen, cost, demand, price, cap, held)
    arrived = everywhere(send, "net")
    parts, dual, mean = call(
        second_body,
        "second",
        shape((net, hours, rows), BF16),
        shape((hours, lines), F32),
        shape((hours, 128), F32),
    )(arrived, ptdf, dual, limit, unit_flow, row_sum)
    arrived = everywhere(parts, "net")
    send, trial = call(
        last_trial_body, "last_trial", shape((net, 8, 128), F32), shape((hours, rows), F32)
    )(arrived, trial, mean, cost, demand, price, cap, held)
    arrived = everywhere(send, "net")
    gen, storage_next, running, price, last = call(
        finish_body,
        "finish",
        shape((hours, rows), F32),
        shape((hours, units), F32),
        shape((hours, units), F32),
        shape((1, hours), F32),
        shape((8, units), F32),
    )(arrived, trial, mean, price, hour_price, held, wear, growth)
    pair = lax.all_gather(last, "tm_1")
    (send,) = call(chip_body, "chip", shape((chips, 8, units), F32))(pair, growth)
    arrived = everywhere(send, "tm_0")
    results = (gen, storage_next, dual, price)
    charge, gen, storage_next, dual, price = pl.pallas_call(
        charge_body,
        name="charge",
        out_specs=[hbm] * 5,
        out_shape=[jax.ShapeDtypeStruct((hours, units), F32)]
        + [jax.ShapeDtypeStruct(a.shape, F32) for a in results],
        scratch_shapes=[pltpu.VMEM((hours, units), F32), pltpu.SemaphoreType.DMA((5,))],
        compiler_params=pltpu.CompilerParams(vmem_limit_bytes=VMEM_LIMIT),
    )(arrived, pair, growth, chain, running, *results)
    return (gen.T, storage_next.T, charge.T, dual.T, price[0])


def solution(mesh):
    split = Mesh(mesh.devices.reshape(16, 2, mesh.shape["net"]), ("tm_0", "tm_1", "net"))
    in_specs = (
        P("net", None),
        P("net", TM),
        P("net", TM),
        P("net", TM),
        P("net"),
        P("net", TM),
        P("net"),
        P("net"),
        P("net"),
        P("net", TM),
        P("net"),
        P(),
        P(),
        P(TM),
        P(TM),
        P(),
    )
    out_specs = (P("net", TM), P("net", TM), P("net", TM), P("net", TM), P(TM))
    return jax.shard_map(
        per_device, mesh=split, in_specs=in_specs, out_specs=out_specs, check_vma=False
    )
```

```python
import jax
import jax.numpy as jnp
from jax import lax
from jax.experimental import pallas as pl
from jax.experimental.pallas import tpu as pltpu
from jax.sharding import Mesh
from jax.sharding import PartitionSpec as P

TM = ("tm_0", "tm_1")

STEP = 0.1
BAL = 0.5
STEP_UNIT = 0.2
ETA = 0.0625

F32 = jnp.float32
VMEM_LIMIT = 16 << 20
BF16 = jnp.bfloat16
NT = (((1,), (1,)), ((), ()))


def call(kernel, name, *outs):
    return pl.pallas_call(
        kernel,
        name=name,
        out_shape=tuple(jax.ShapeDtypeStruct(s, d) for s, d in outs),
        compiler_params=pltpu.CompilerParams(vmem_limit_bytes=VMEM_LIMIT),
    )


def shape(s, d):
    return s, d


def iota(dims, axis):
    return lax.broadcasted_iota(jnp.int32, dims, axis)


def column(row, n):
    eye = iota((n, n), 0) == iota((n, n), 1)
    return jnp.sum(jnp.where(eye, row[:, :n], jnp.zeros((), row.dtype)), axis=1, keepdims=True)


def row_of(col, width):
    n = col.shape[0]
    eye = iota((n, width), 0) == iota((n, width), 1)
    return jnp.sum(jnp.where(eye, col, 0.0), axis=0, keepdims=True)


def three_parts(value):
    high = value.astype(BF16)
    rest = value - high.astype(F32)
    middle = rest.astype(BF16)
    low = (rest - middle.astype(F32)).astype(BF16)
    return high, middle, low


def pack_body(
    chip, core, gen_in, demand_in, storage_in, bus_in, dual_in, rating_in, index_in, leakage_in,
    block_in, prices_in, initial_in,
    out, limit, growth, hour_price, chain, bus, line_dual,
    gen, demand, storage, rating, index, leakage, hour_block, block_price, initial, sems
):
    pairs = (
        (gen_in, gen),
        (demand_in, demand),
        (storage_in, storage),
        (rating_in, rating),
        (index_in, index),
        (leakage_in, leakage),
        (block_in, hour_block),
        (prices_in, block_price),
        (initial_in, initial),
        (bus_in, bus),
        (dual_in, line_dual),
    )
    copies = [pltpu.make_async_copy(a, b, sems.at[k]) for k, (a, b) in enumerate(pairs)]
    for copy in copies:
        copy.start()
    for copy in copies[:3]:
        copy.wait()
    rows = gen.shape[1]
    injection = (gen[...] - demand[...]).astype(BF16)
    units = storage[...].astype(BF16)
    for d in range(out.shape[0]):
        out[d, :, :rows] = injection
        out[d, :, rows:] = units
    for copy in copies[3:]:
        copy.wait()
    here = chip[0], core[0]
    write_tables(
        here, rating, index, leakage, hour_block, block_price, initial, limit, growth, hour_price, chain
    )


def write_tables(
    here, rating, index, leakage, hour_block, block_price, initial, limit, growth, hour_price, chain
):
    groups = rating.shape[0]
    at = index[...]
    hot = (iota((groups, at.shape[1]), 0) == at // 128).astype(BF16)
    table = rating[...].T
    picked = sum(jnp.dot(part, hot, preferred_element_type=F32) for part in three_parts(table))
    found = iota((128, at.shape[1]), 0) == at % 128
    limit[...] = jnp.sum(jnp.where(found, picked, 0.0), axis=0, keepdims=True)
    hours, units = growth.shape
    offsets = (iota((hours, units), 0) + 1).astype(F32)
    rate = jnp.log(1.0 - leakage[...])
    growth[...] = jnp.exp(offsets * rate)
    count = chain.shape[0] - 8
    row = iota(chain.shape, 0)
    spans = jnp.where(row < count, 2 * (here[0] - 1 - row), 2 * here[0]) + here[1]
    weight = jnp.exp((jnp.maximum(spans, 0) * hours).astype(F32) * rate)
    weight = jnp.where((row < here[0]) | (row == count), weight, 0.0)
    weight = jnp.where(row == count, weight * initial[...], weight)
    chain[...] = jnp.where(row == count + 1, here[1].astype(F32), weight)
    block = column(hour_block[...], hours)
    blocks = block_price.shape[1]
    price = jnp.where(block == iota((hours, blocks), 1), block_price[...], 0.0)
    hour_price[...] = jnp.broadcast_to(jnp.sum(price, axis=1, keepdims=True), hour_price.shape)


def clipped(flows, dual, limit):
    shifted = flows + dual
    return shifted - jnp.clip(shifted, -limit, limit)


def pull_parts(dual, ptdf, out):
    pull = jnp.dot(dual.astype(BF16), ptdf[...], preferred_element_type=F32)
    rows = out.shape[2]
    for d in range(out.shape[0]):
        out[d] = pull[:, d * rows : (d + 1) * rows].astype(BF16)


def first_body(
    arrived, ptdf, bus, line_dual, limit, parts, dual_out, unit_flow_out, row_sum, held,
    lefts, owned, hot, sem
):
    copy = pltpu.make_async_copy(ptdf, held, sem)
    copy.start()
    count, hours, width = arrived.shape
    rows = parts.shape[2]
    units = width - rows
    for d in range(count):
        at = slice(d * rows, (d + 1) * rows)
        lefts[:hours, at] = arrived[d, :, :rows]
        lefts[3 * hours :, at] = (iota((count, rows), 0) == d).astype(F32).astype(BF16)
    owner, place = bus[...] // rows, bus[...] % rows
    bus_row = iota((rows, units), 0)
    for k in range(count):
        at = slice(k * units, (k + 1) * units)
        hot[:, at] = (bus_row == place[:, at]).astype(F32).astype(BF16)
        for d in range(count):
            mine = jnp.broadcast_to((owner[:, at] == d).astype(F32), (16, units)).astype(BF16)
            for h in range(0, hours, 16):
                owned[d * hours + h : d * hours + h + 16, at] = arrived[k, h : h + 16, rows:] * mine
    spread = lax.dot_general(owned[...], hot[...], NT, preferred_element_type=F32)
    for d in range(count):
        part = spread[d * hours : (d + 1) * hours]
        high = part.astype(BF16)
        at = slice(d * rows, (d + 1) * rows)
        lefts[hours : 2 * hours, at] = high
        lefts[2 * hours : 3 * hours, at] = (part - high.astype(F32)).astype(BF16)
    copy.wait()
    products = lax.dot_general(lefts[...], held[...], NT, preferred_element_type=F32)
    unit_flow = products[hours : 2 * hours] + products[2 * hours : 3 * hours]
    row_sum[...] = products[3 * hours :]
    unit_flow_out[...] = unit_flow
    dual = clipped(products[:hours] + unit_flow, line_dual[...], limit[...])
    dual_out[...] = dual
    pull_parts(dual, held, parts)


def second_body(arrived, ptdf, line_dual, limit, unit_flow, row_sum, parts, dual_out, mean_out):
    count, hours, rows = parts.shape
    notes = jnp.concatenate([arrived[d, hours : hours + 8] for d in range(count)], axis=0)
    notes = notes.astype(F32)
    notes = notes[:, :hours] + notes[:, hours : 2 * hours] + notes[:, 2 * hours : 3 * hours]
    means = jnp.concatenate([notes[8 * d : 8 * d + 1] for d in range(count)], axis=0)
    units = jnp.concatenate([notes[8 * d + 1 : 8 * d + 2] for d in range(count)], axis=0)
    mean = jnp.sum(means * rows + units, axis=0, keepdims=True) / (count * rows)
    mean_out[...] = jnp.broadcast_to(column(mean, hours), mean_out.shape)
    balance = jnp.concatenate([arrived[d, :hours] for d in range(count)], axis=1)
    flows = lax.dot_general(balance, ptdf[...], NT, preferred_element_type=F32)
    flows += lax.dot_general(
        means - mean,
        row_sum[...],
        (((0,), (0,)), ((), ())),
        precision=lax.Precision.HIGHEST,
        preferred_element_type=F32,
    )
    dual = clipped(flows + unit_flow[...], line_dual[...], limit[...])
    dual_out[...] = dual
    pull_parts(dual, ptdf, parts)


def note(col, width):
    n = col.shape[0]
    high, middle, low = (part.astype(F32) for part in three_parts(col))
    lane = iota((n, width), 1)
    value = jnp.where(lane < n, high, jnp.where(lane < 2 * n, middle, low))
    mine = (lane % n == iota((n, width), 0)) & (lane < 3 * n)
    return jnp.sum(jnp.where(mine, value, 0.0), axis=0, keepdims=True)


def total_of(arrived):
    total = arrived[0].astype(F32)
    for d in range(1, arrived.shape[0]):
        total += arrived[d].astype(F32)
    return total


def trial_body(arrived, gen, cost, demand, price, cap, storage, send, trial_out):
    hours = gen.shape[0]
    pull = total_of(arrived)
    now = column(price[...], hours)
    trial = jnp.clip(gen[...] - STEP * (cost[...] - now + pull), 0.0, cap[...])
    trial_out[...] = trial
    balance = trial - demand[...]
    width = balance.shape[1]
    mean = jnp.sum(balance, axis=1, keepdims=True) / width
    unit_sum = jnp.sum(storage[...], axis=1, keepdims=True)
    row = iota((8, width), 0)
    below = jnp.where(row == 0, note(mean, width), jnp.where(row == 1, note(unit_sum, width), 0.0))
    below = below.astype(BF16)
    around = (balance - mean).astype(BF16)
    for d in range(send.shape[0]):
        send[d, :hours] = around
        send[d, hours:] = below


def last_trial_body(arrived, before, mean, cost, demand, price, cap, storage, send, trial_out):
    hours = before.shape[0]
    pull = total_of(arrived)
    moved = mean[:, :1]
    now = column(price[...], hours) - BAL * moved
    trial = jnp.clip(before[...] - moved - STEP * (cost[...] - now + pull), 0.0, cap[...])
    trial_out[...] = trial
    own = jnp.sum(trial - demand[...], axis=1, keepdims=True)
    own += jnp.sum(storage[...], axis=1, keepdims=True)
    send[...] = jnp.broadcast_to(row_of(own, send.shape[2])[None], send.shape)


def finish_body(
    arrived, trial, mean, price, hour_price, storage, wear, growth, gen_out, storage_out, running_out, price_out, last_out
):
    hours, units = storage.shape
    buses = arrived.shape[0] * trial.shape[1]
    mismatch = column(total_of(arrived)[:1], hours) / buses
    gen_out[...] = trial[...] - mismatch
    now = column(price[...], hours) - BAL * mean[:, :1] - BAL * mismatch
    price_out[...] = row_of(now, price_out.shape[1])
    held = storage[...]
    nexts = jnp.clip(held + STEP_UNIT * (now + hour_price[...] - wear[...] * held), -1.0, 1.0)
    storage_out[...] = nexts
    running = -ETA * nexts
    hour = iota((hours, units), 0)
    span = 1
    while span < hours:
        moved = jnp.where(hour >= span, pltpu.roll(running, span, 0), 0.0)
        running = running + growth[span - 1 : span] * moved
        span *= 2
    running_out[...] = running
    last_out[...] = jnp.broadcast_to(running[hours - 1 :], last_out.shape)


def chip_body(pair, growth, send):
    hours = growth.shape[0]
    both = growth[hours - 1 :] * pair[0] + pair[1]
    send[...] = jnp.broadcast_to(both[None], send.shape)


def charge_body(
    arrived, pair, growth, chain, running, gen, storage, dual, price,
    charge_out, gen_out, storage_out, dual_out, price_out, charge, sems
):
    done = ((gen, gen_out), (storage, storage_out), (dual, dual_out), (price, price_out))
    copies = [pltpu.make_async_copy(a, b, sems.at[k]) for k, (a, b) in enumerate(done)]
    for copy in copies:
        copy.start()
    count = arrived.shape[0]
    entering = chain[count : count + 1] + chain[count + 1 : count + 2] * pair[0, :1]
    for k in range(count):
        entering += chain[k : k + 1] * arrived[k, :1]
    charge[...] = growth[...] * entering + running[...]
    last = pltpu.make_async_copy(charge, charge_out, sems.at[len(done)])
    last.start()
    for copy in copies:
        copy.wait()
    last.wait()


def in_hbm(array):
    return pltpu.with_memory_space_constraint(array, pltpu.HBM)


def everywhere(blocks, axis):
    return lax.all_to_all(blocks, axis, split_axis=0, concat_axis=0, tiled=True)


def per_device(
    ptdf,
    demand,
    generation,
    cost,
    gen_cap,
    storage,
    wear,
    initial_charge,
    leakage,
    line_dual,
    line_index,
    rating,
    storage_bus,
    balance_dual,
    hour_block,
    block_price,
):
    net = lax.axis_size("net")
    chips = lax.axis_size("tm_0")
    lines = ptdf.shape[0]
    rows, hours = generation.shape
    units = storage.shape[0]
    demand, gen, cost, held = demand.T, generation.T, cost.T, storage.T
    dual = line_dual.T
    cap, wear, initial = gen_cap[None], wear[None], initial_charge[None]
    price = balance_dual[None]
    chip, core, gen = lax.optimization_barrier(
        (lax.axis_index("tm_0").reshape(1), lax.axis_index("tm_1").reshape(1), gen)
    )
    sources = (
        gen,
        demand,
        held,
        storage_bus[None],
        dual,
        rating.reshape(-1, 128),
        line_index[None],
        leakage[None],
        hour_block[None],
        block_price[None],
        initial,
    )
    smem, hbm = (pl.BlockSpec(memory_space=m) for m in (pltpu.SMEM, pltpu.HBM))
    packed, limit, growth, hour_price, chain, bus, dual = pl.pallas_call(
        pack_body,
        name="pack",
        in_specs=[smem, smem] + [hbm] * len(sources),
        out_shape=(
            jax.ShapeDtypeStruct((net, hours, rows + units), BF16),
            jax.ShapeDtypeStruct((1, lines), F32),
            jax.ShapeDtypeStruct((hours, units), F32),
            jax.ShapeDtypeStruct((hours, units), F32),
            jax.ShapeDtypeStruct((chips + 8, units), F32),
            jax.ShapeDtypeStruct((1, net * units), jnp.int32),
            jax.ShapeDtypeStruct((hours, lines), F32),
        ),
        scratch_shapes=[
            *(pltpu.VMEM(a.shape, a.dtype) for a in sources[:3] + sources[5:]),
            pltpu.SemaphoreType.DMA((len(sources),)),
        ],
        compiler_params=pltpu.CompilerParams(vmem_limit_bytes=VMEM_LIMIT),
    )(chip, core, *(in_hbm(a) for a in sources))
    arrived = everywhere(packed, "net")
    parts, dual, unit_flow, row_sum, ptdf = pl.pallas_call(
        first_body,
        name="first",
        in_specs=[pl.BlockSpec(), hbm] + [pl.BlockSpec()] * 3,
        out_shape=(
            jax.ShapeDtypeStruct((net, hours, rows), BF16),
            jax.ShapeDtypeStruct((hours, lines), F32),
            jax.ShapeDtypeStruct((hours, lines), F32),
            jax.ShapeDtypeStruct((net, lines), F32),
            jax.ShapeDtypeStruct(ptdf.shape, BF16),
        ),
        scratch_shapes=[
            pltpu.VMEM((3 * hours + net, net * rows), BF16),
            pltpu.VMEM((net * hours, net * units), BF16),
            pltpu.VMEM((rows, net * units), BF16),
            pltpu.SemaphoreType.DMA(()),
        ],
        compiler_params=pltpu.CompilerParams(vmem_limit_bytes=VMEM_LIMIT),
    )(arrived, in_hbm(ptdf), bus, dual, limit)
    arrived = everywhere(parts, "net")
    send, trial = call(
        trial_body, "trial", shape((net, hours + 8, rows), BF16), shape((hours, rows), F32)
    )(arrived, gen, cost, demand, price, cap, held)
    arrived = everywhere(send, "net")
    parts, dual, mean = call(
        second_body,
        "second",
        shape((net, hours, rows), BF16),
        shape((hours, lines), F32),
        shape((hours, 128), F32),
    )(arrived, ptdf, dual, limit, unit_flow, row_sum)
    arrived = everywhere(parts, "net")
    send, trial = call(
        last_trial_body, "last_trial", shape((net, 8, 128), F32), shape((hours, rows), F32)
    )(arrived, trial, mean, cost, demand, price, cap, held)
    arrived = everywhere(send, "net")
    gen, storage_next, running, price, last = call(
        finish_body,
        "finish",
        shape((hours, rows), F32),
        shape((hours, units), F32),
        shape((hours, units), F32),
        shape((1, hours), F32),
        shape((8, units), F32),
    )(arrived, trial, mean, price, hour_price, held, wear, growth)
    pair = lax.all_gather(last, "tm_1")
    (send,) = call(chip_body, "chip", shape((chips, 8, units), F32))(pair, growth)
    arrived = everywhere(send, "tm_0")
    results = (gen, storage_next, dual, price)
    charge, gen, storage_next, dual, price = pl.pallas_call(
        charge_body,
        name="charge",
        out_specs=[hbm] * 5,
        out_shape=[jax.ShapeDtypeStruct((hours, units), F32)]
        + [jax.ShapeDtypeStruct(a.shape, F32) for a in results],
        scratch_shapes=[pltpu.VMEM((hours, units), F32), pltpu.SemaphoreType.DMA((5,))],
        compiler_params=pltpu.CompilerParams(vmem_limit_bytes=VMEM_LIMIT),
    )(arrived, pair, growth, chain, running, *results)
    return (gen.T, storage_next.T, charge.T, dual.T, price[0])


def solution(mesh):
    split = Mesh(mesh.devices.reshape(16, 2, mesh.shape["net"]), ("tm_0", "tm_1", "net"))
    in_specs = (
        P("net", None),
        P("net", TM),
        P("net", TM),
        P("net", TM),
        P("net"),
        P("net", TM),
        P("net"),
        P("net"),
        P("net"),
        P("net", TM),
        P("net"),
        P(),
        P(),
        P(TM),
        P(TM),
        P(),
    )
    out_specs = (P("net", TM), P("net", TM), P("net", TM), P("net", TM), P(TM))
    return jax.shard_map(
        per_device, mesh=split, in_specs=in_specs, out_specs=out_specs, check_vma=False
    )
```

```python
import jax
import jax.numpy as jnp
from jax import lax
from jax.experimental import pallas as pl
from jax.experimental.pallas import tpu as pltpu
from jax.sharding import Mesh
from jax.sharding import PartitionSpec as P

TM = ("tm_0", "tm_1")

STEP = 0.1
BAL = 0.5
STEP_UNIT = 0.2
ETA = 0.0625

F32 = jnp.float32
VMEM_LIMIT = 16 << 20
BF16 = jnp.bfloat16
NT = (((1,), (1,)), ((), ()))


def call(kernel, name, *outs):
    return pl.pallas_call(
        kernel,
        name=name,
        out_shape=tuple(jax.ShapeDtypeStruct(s, d) for s, d in outs),
        compiler_params=pltpu.CompilerParams(vmem_limit_bytes=VMEM_LIMIT),
    )


def shape(s, d):
    return s, d


def iota(dims, axis):
    return lax.broadcasted_iota(jnp.int32, dims, axis)


def column(row, n):
    eye = iota((n, n), 0) == iota((n, n), 1)
    return jnp.sum(jnp.where(eye, row[:, :n], jnp.zeros((), row.dtype)), axis=1, keepdims=True)


def row_of(col, width):
    n = col.shape[0]
    eye = iota((n, width), 0) == iota((n, width), 1)
    return jnp.sum(jnp.where(eye, col, 0.0), axis=0, keepdims=True)


def three_parts(value):
    high = value.astype(BF16)
    rest = value - high.astype(F32)
    middle = rest.astype(BF16)
    low = (rest - middle.astype(F32)).astype(BF16)
    return high, middle, low


def pack_body(
    gen_in, demand_in, storage_in, bus_in, out, bus, gen, demand, storage, sems
):
    pairs = ((gen_in, gen), (demand_in, demand), (storage_in, storage), (bus_in, bus))
    copies = [pltpu.make_async_copy(a, b, sems.at[k]) for k, (a, b) in enumerate(pairs)]
    for copy in copies:
        copy.start()
    for copy in copies[:3]:
        copy.wait()
    rows = gen.shape[1]
    injection = (gen[...] - demand[...]).astype(BF16)
    units = storage[...].astype(BF16)
    for d in range(out.shape[0]):
        out[d, :, :rows] = injection
        out[d, :, rows:] = units
    for copy in copies[3:]:
        copy.wait()


def write_tables(
    here, rating, index, leakage, hour_block, block_price, initial, limit, growth, hour_price, chain
):
    groups = rating.shape[0]
    at = index[...]
    hot = (iota((groups, at.shape[1]), 0) == at // 128).astype(BF16)
    table = rating[...].T
    picked = sum(jnp.dot(part, hot, preferred_element_type=F32) for part in three_parts(table))
    found = iota((128, at.shape[1]), 0) == at % 128
    limit[...] = jnp.sum(jnp.where(found, picked, 0.0), axis=0, keepdims=True)
    hours, units = growth.shape
    offsets = (iota((hours, units), 0) + 1).astype(F32)
    rate = jnp.log(1.0 - leakage[...])
    growth[...] = jnp.exp(offsets * rate)
    count = chain.shape[0] - 8
    row = iota(chain.shape, 0)
    spans = jnp.where(row < count, 2 * (here[0] - 1 - row), 2 * here[0]) + here[1]
    weight = jnp.exp((jnp.maximum(spans, 0) * hours).astype(F32) * rate)
    weight = jnp.where((row < here[0]) | (row == count), weight, 0.0)
    weight = jnp.where(row == count, weight * initial[...], weight)
    chain[...] = jnp.where(row == count + 1, here[1].astype(F32), weight)
    block = column(hour_block[...], hours)
    blocks = block_price.shape[1]
    price = jnp.where(block == iota((hours, blocks), 1), block_price[...], 0.0)
    hour_price[...] = jnp.broadcast_to(jnp.sum(price, axis=1, keepdims=True), hour_price.shape)


def clipped(flows, dual, limit):
    shifted = flows + dual
    return shifted - jnp.clip(shifted, -limit, limit)


def pull_parts(dual, ptdf, out):
    pull = jnp.dot(dual.astype(BF16), ptdf[...], preferred_element_type=F32)
    rows = out.shape[2]
    for d in range(out.shape[0]):
        out[d] = pull[:, d * rows : (d + 1) * rows].astype(BF16)


def first_body(
    chip, core, arrived, bus, ptdf, dual_in, rating_in, index_in, leakage_in, block_in, prices_in, initial_in,
    parts, dual_out, unit_flow_out, row_sum, limit, growth, hour_price, chain, held,
    line_dual, rating, index, leakage, hour_block, block_price, initial, lefts, owned, hot, sem, sems
):
    pairs = (
        (rating_in, rating),
        (index_in, index),
        (leakage_in, leakage),
        (block_in, hour_block),
        (prices_in, block_price),
        (initial_in, initial),
        (dual_in, line_dual),
    )
    small = [pltpu.make_async_copy(a, b, sems.at[k]) for k, (a, b) in enumerate(pairs)]
    for each in small:
        each.start()
    copy = pltpu.make_async_copy(ptdf, held, sem)
    copy.start()
    count, hours, width = arrived.shape
    rows = parts.shape[2]
    units = width - rows
    for d in range(count):
        at = slice(d * rows, (d + 1) * rows)
        lefts[:hours, at] = arrived[d, :, :rows]
        lefts[3 * hours :, at] = (iota((count, rows), 0) == d).astype(F32).astype(BF16)
    owner, place = bus[...] // rows, bus[...] % rows
    bus_row = iota((rows, units), 0)
    for k in range(count):
        at = slice(k * units, (k + 1) * units)
        hot[:, at] = (bus_row == place[:, at]).astype(F32).astype(BF16)
        for d in range(count):
            mine = jnp.broadcast_to((owner[:, at] == d).astype(F32), (16, units)).astype(BF16)
            for h in range(0, hours, 16):
                owned[d * hours + h : d * hours + h + 16, at] = arrived[k, h : h + 16, rows:] * mine
    spread = lax.dot_general(owned[...], hot[...], NT, preferred_element_type=F32)
    for d in range(count):
        part = spread[d * hours : (d + 1) * hours]
        high = part.astype(BF16)
        at = slice(d * rows, (d + 1) * rows)
        lefts[hours : 2 * hours, at] = high
        lefts[2 * hours : 3 * hours, at] = (part - high.astype(F32)).astype(BF16)
    for each in small:
        each.wait()
    here = chip[0], core[0]
    write_tables(
        here, rating, index, leakage, hour_block, block_price, initial, limit, growth, hour_price, chain
    )
    copy.wait()
    products = lax.dot_general(lefts[...], held[...], NT, preferred_element_type=F32)
    unit_flow = products[hours : 2 * hours] + products[2 * hours : 3 * hours]
    row_sum[...] = products[3 * hours :]
    unit_flow_out[...] = unit_flow
    dual = clipped(products[:hours] + unit_flow, line_dual[...], limit[...])
    dual_out[...] = dual
    pull_parts(dual, held, parts)


def second_body(arrived, ptdf, line_dual, limit, unit_flow, row_sum, parts, dual_out, mean_out):
    count, hours, rows = parts.shape
    notes = jnp.concatenate([arrived[d, hours : hours + 8] for d in range(count)], axis=0)
    notes = notes.astype(F32)
    notes = notes[:, :hours] + notes[:, hours : 2 * hours] + notes[:, 2 * hours : 3 * hours]
    means = jnp.concatenate([notes[8 * d : 8 * d + 1] for d in range(count)], axis=0)
    units = jnp.concatenate([notes[8 * d + 1 : 8 * d + 2] for d in range(count)], axis=0)
    mean = jnp.sum(means * rows + units, axis=0, keepdims=True) / (count * rows)
    mean_out[...] = jnp.broadcast_to(column(mean, hours), mean_out.shape)
    balance = jnp.concatenate([arrived[d, :hours] for d in range(count)], axis=1)
    flows = lax.dot_general(balance, ptdf[...], NT, preferred_element_type=F32)
    flows += lax.dot_general(
        means - mean,
        row_sum[...],
        (((0,), (0,)), ((), ())),
        precision=lax.Precision.HIGHEST,
        preferred_element_type=F32,
    )
    dual = clipped(flows + unit_flow[...], line_dual[...], limit[...])
    dual_out[...] = dual
    pull_parts(dual, ptdf, parts)


def note(col, width):
    n = col.shape[0]
    high, middle, low = (part.astype(F32) for part in three_parts(col))
    lane = iota((n, width), 1)
    value = jnp.where(lane < n, high, jnp.where(lane < 2 * n, middle, low))
    mine = (lane % n == iota((n, width), 0)) & (lane < 3 * n)
    return jnp.sum(jnp.where(mine, value, 0.0), axis=0, keepdims=True)


def total_of(arrived):
    total = arrived[0].astype(F32)
    for d in range(1, arrived.shape[0]):
        total += arrived[d].astype(F32)
    return total


def trial_body(arrived, gen, cost, demand, price, cap, storage, send, trial_out):
    hours = gen.shape[0]
    pull = total_of(arrived)
    now = column(price[...], hours)
    trial = jnp.clip(gen[...] - STEP * (cost[...] - now + pull), 0.0, cap[...])
    trial_out[...] = trial
    balance = trial - demand[...]
    width = balance.shape[1]
    mean = jnp.sum(balance, axis=1, keepdims=True) / width
    unit_sum = jnp.sum(storage[...], axis=1, keepdims=True)
    row = iota((8, width), 0)
    below = jnp.where(row == 0, note(mean, width), jnp.where(row == 1, note(unit_sum, width), 0.0))
    below = below.astype(BF16)
    around = (balance - mean).astype(BF16)
    for d in range(send.shape[0]):
        send[d, :hours] = around
        send[d, hours:] = below


def last_trial_body(arrived, before, mean, cost, demand, price, cap, storage, send, trial_out):
    hours = before.shape[0]
    pull = total_of(arrived)
    moved = mean[:, :1]
    now = column(price[...], hours) - BAL * moved
    trial = jnp.clip(before[...] - moved - STEP * (cost[...] - now + pull), 0.0, cap[...])
    trial_out[...] = trial
    own = jnp.sum(trial - demand[...], axis=1, keepdims=True)
    own += jnp.sum(storage[...], axis=1, keepdims=True)
    send[...] = jnp.broadcast_to(row_of(own, send.shape[2])[None], send.shape)


def finish_body(
    arrived, trial, mean, price, hour_price, storage, wear, growth, gen_out, storage_out, running_out, price_out, last_out
):
    hours, units = storage.shape
    buses = arrived.shape[0] * trial.shape[1]
    mismatch = column(total_of(arrived)[:1], hours) / buses
    gen_out[...] = trial[...] - mismatch
    now = column(price[...], hours) - BAL * mean[:, :1] - BAL * mismatch
    price_out[...] = row_of(now, price_out.shape[1])
    held = storage[...]
    nexts = jnp.clip(held + STEP_UNIT * (now + hour_price[...] - wear[...] * held), -1.0, 1.0)
    storage_out[...] = nexts
    running = -ETA * nexts
    hour = iota((hours, units), 0)
    span = 1
    while span < hours:
        moved = jnp.where(hour >= span, pltpu.roll(running, span, 0), 0.0)
        running = running + growth[span - 1 : span] * moved
        span *= 2
    running_out[...] = running
    last_out[...] = jnp.broadcast_to(running[hours - 1 :], last_out.shape)


def chip_body(pair, growth, send):
    hours = growth.shape[0]
    both = growth[hours - 1 :] * pair[0] + pair[1]
    send[...] = jnp.broadcast_to(both[None], send.shape)


def charge_body(
    arrived, pair, growth, chain, running, gen, storage, dual, price,
    charge_out, gen_out, storage_out, dual_out, price_out, charge, sems
):
    done = ((gen, gen_out), (storage, storage_out), (dual, dual_out), (price, price_out))
    copies = [pltpu.make_async_copy(a, b, sems.at[k]) for k, (a, b) in enumerate(done)]
    for copy in copies:
        copy.start()
    count = arrived.shape[0]
    entering = chain[count : count + 1] + chain[count + 1 : count + 2] * pair[0, :1]
    for k in range(count):
        entering += chain[k : k + 1] * arrived[k, :1]
    charge[...] = growth[...] * entering + running[...]
    last = pltpu.make_async_copy(charge, charge_out, sems.at[len(done)])
    last.start()
    for copy in copies:
        copy.wait()
    last.wait()


def in_hbm(array):
    return pltpu.with_memory_space_constraint(array, pltpu.HBM)


def everywhere(blocks, axis):
    return lax.all_to_all(blocks, axis, split_axis=0, concat_axis=0, tiled=True)


def per_device(
    ptdf,
    demand,
    generation,
    cost,
    gen_cap,
    storage,
    wear,
    initial_charge,
    leakage,
    line_dual,
    line_index,
    rating,
    storage_bus,
    balance_dual,
    hour_block,
    block_price,
):
    net = lax.axis_size("net")
    chips = lax.axis_size("tm_0")
    lines = ptdf.shape[0]
    rows, hours = generation.shape
    units = storage.shape[0]
    demand, gen, cost, held = demand.T, generation.T, cost.T, storage.T
    dual = line_dual.T
    cap, wear, initial = gen_cap[None], wear[None], initial_charge[None]
    price = balance_dual[None]
    chip, core, gen = lax.optimization_barrier(
        (lax.axis_index("tm_0").reshape(1), lax.axis_index("tm_1").reshape(1), gen)
    )
    sources = (gen, demand, held, storage_bus[None])
    smem, hbm = (pl.BlockSpec(memory_space=m) for m in (pltpu.SMEM, pltpu.HBM))
    packed, bus = pl.pallas_call(
        pack_body,
        name="pack",
        in_specs=[hbm] * len(sources),
        out_shape=(
            jax.ShapeDtypeStruct((net, hours, rows + units), BF16),
            jax.ShapeDtypeStruct((1, net * units), jnp.int32),
        ),
        scratch_shapes=[
            *(pltpu.VMEM(a.shape, a.dtype) for a in sources[:3]),
            pltpu.SemaphoreType.DMA((len(sources),)),
        ],
        compiler_params=pltpu.CompilerParams(vmem_limit_bytes=VMEM_LIMIT),
    )(*(in_hbm(a) for a in sources))
    arrived = everywhere(packed, "net")
    sources = (
        rating.reshape(-1, 128),
        line_index[None],
        leakage[None],
        hour_block[None],
        block_price[None],
        initial,
    )
    parts, dual, unit_flow, row_sum, limit, growth, hour_price, chain, ptdf = pl.pallas_call(
        first_body,
        name="first",
        in_specs=[smem, smem, pl.BlockSpec(), pl.BlockSpec()] + [hbm] * 8,
        out_shape=(
            jax.ShapeDtypeStruct((net, hours, rows), BF16),
            jax.ShapeDtypeStruct((hours, lines), F32),
            jax.ShapeDtypeStruct((hours, lines), F32),
            jax.ShapeDtypeStruct((net, lines), F32),
            jax.ShapeDtypeStruct((1, lines), F32),
            jax.ShapeDtypeStruct((hours, units), F32),
            jax.ShapeDtypeStruct((hours, units), F32),
            jax.ShapeDtypeStruct((chips + 8, units), F32),
            jax.ShapeDtypeStruct(ptdf.shape, BF16),
        ),
        scratch_shapes=[
            *(pltpu.VMEM(a.shape, a.dtype) for a in (dual, *sources)),
            pltpu.VMEM((3 * hours + net, net * rows), BF16),
            pltpu.VMEM((net * hours, net * units), BF16),
            pltpu.VMEM((rows, net * units), BF16),
            pltpu.SemaphoreType.DMA(()),
            pltpu.SemaphoreType.DMA((7,)),
        ],
        compiler_params=pltpu.CompilerParams(vmem_limit_bytes=VMEM_LIMIT),
    )(chip, core, arrived, bus, *(in_hbm(a) for a in (ptdf, dual, *sources)))
    arrived = everywhere(parts, "net")
    send, trial = call(
        trial_body, "trial", shape((net, hours + 8, rows), BF16), shape((hours, rows), F32)
    )(arrived, gen, cost, demand, price, cap, held)
    arrived = everywhere(send, "net")
    parts, dual, mean = call(
        second_body,
        "second",
        shape((net, hours, rows), BF16),
        shape((hours, lines), F32),
        shape((hours, 128), F32),
    )(arrived, ptdf, dual, limit, unit_flow, row_sum)
    arrived = everywhere(parts, "net")
    send, trial = call(
        last_trial_body, "last_trial", shape((net, 8, 128), F32), shape((hours, rows), F32)
    )(arrived, trial, mean, cost, demand, price, cap, held)
    arrived = everywhere(send, "net")
    gen, storage_next, running, price, last = call(
        finish_body,
        "finish",
        shape((hours, rows), F32),
        shape((hours, units), F32),
        shape((hours, units), F32),
        shape((1, hours), F32),
        shape((8, units), F32),
    )(arrived, trial, mean, price, hour_price, held, wear, growth)
    pair = lax.all_gather(last, "tm_1")
    (send,) = call(chip_body, "chip", shape((chips, 8, units), F32))(pair, growth)
    arrived = everywhere(send, "tm_0")
    results = (gen, storage_next, dual, price)
    charge, gen, storage_next, dual, price = pl.pallas_call(
        charge_body,
        name="charge",
        out_specs=[hbm] * 5,
        out_shape=[jax.ShapeDtypeStruct((hours, units), F32)]
        + [jax.ShapeDtypeStruct(a.shape, F32) for a in results],
        scratch_shapes=[pltpu.VMEM((hours, units), F32), pltpu.SemaphoreType.DMA((5,))],
        compiler_params=pltpu.CompilerParams(vmem_limit_bytes=VMEM_LIMIT),
    )(arrived, pair, growth, chain, running, *results)
    return (gen.T, storage_next.T, charge.T, dual.T, price[0])


def solution(mesh):
    split = Mesh(mesh.devices.reshape(16, 2, mesh.shape["net"]), ("tm_0", "tm_1", "net"))
    in_specs = (
        P("net", None),
        P("net", TM),
        P("net", TM),
        P("net", TM),
        P("net"),
        P("net", TM),
        P("net"),
        P("net"),
        P("net"),
        P("net", TM),
        P("net"),
        P(),
        P(),
        P(TM),
        P(TM),
        P(),
    )
    out_specs = (P("net", TM), P("net", TM), P("net", TM), P("net", TM), P(TM))
    return jax.shard_map(
        per_device, mesh=split, in_specs=in_specs, out_specs=out_specs, check_vma=False
    )
```
